32 devices in a mesh: scene: 8 (over z, x), tie: 4 (over y, core).
Axes of the slice: x: 2, y: 2, z: 4, core: 2. Of those that a mesh axis runs over, the one named last changes fastest.
Arguments:
- tie_rows: bfloat16 [384, 256, 256], P('tie'), may hold values from -0.375 to 0.375
- point_counts: int32 [384], P('tie'), may hold values from 1 to 128, as said below
- pattern: int32 [128, 384], P('scene', 'tie'), may hold values 0 or 1
- sensitivity: bfloat16 [128, 192, 192], P('scene'), may hold values from -0.119628906 to 0.119628906
- damping: float32 [128], P(('scene', 'tie')), may hold values from 1 to 8
- prior: float32 [64], replicated, may hold values from 0.25 to 4
Outputs:
- scene_rows: float32 [128, 192, 256], P(('scene', 'tie'))
- global_factor: float32 [64, 64], replicated
The draws below stay inside these ranges and needn't reach their ends.
Inputs may be any that keep to these rules, and one draw needn't show every extreme that they name: `point_counts`: points present in each block; some block is full.
All inputs are finite; a program needn't handle non-finite values. No bound on the sum of `pattern` on one device may be relied on, other than what follows from the above.
Results may differ from the reference program's by a relative error of at most 0.0003.
Values sent between devices are 32-bit elements; how exact they have to be, the bound alone decides.
A program may use at most 128 MiB of HBM per device.

```python
import math
import jax
import jax.numpy as jnp
from jax import lax

SPLINE = 192
SHARED = 64
COLS = 256
PTS = 128
ROWS = 256
SC_SHARD = 16
NSC = 128
NBLK = 384
N_SCENE = 8


def draw_point_counts(key, part):
    first_key, second_key = jax.random.split(jax.random.fold_in(key, 11))
    counts = jax.random.randint(first_key, (NBLK,), PTS // 4, PTS + 1)
    chosen = jax.random.randint(second_key, (), 0, NBLK)
    return jnp.where(jnp.arange(NBLK) == chosen, PTS, counts).astype(jnp.int32)


def plant(drawn, key, smallest, top_value):
    spot = [jax.random.randint(jax.random.fold_in(key, axis), (), 0, length) for axis, length in enumerate(drawn.shape)]
    main_axis = drawn.shape.index(max(drawn.shape))
    neighbour = spot[:main_axis] + [(spot[main_axis] + 1) % drawn.shape[main_axis]] + spot[main_axis + 1:]
    return drawn.at[tuple(spot)].set(smallest).at[tuple(neighbour)].set(top_value)


def block_levels(stream_key, extent, pieces, least, largest):
    def one(axis_at, shards_of):
        heights = jax.random.uniform(jax.random.fold_in(jax.random.fold_in(stream_key, 6), axis_at), (shards_of,), jnp.float32, least / len(pieces), largest / len(pieces))
        return jnp.repeat(jnp.exp(heights), extent[axis_at] // shards_of).reshape((-1,) + (1,) * (len(extent) - axis_at - 1))

    gain = one(*pieces[0])
    for cut in pieces[1:]:
        gain = gain * one(*cut)
    return gain


def normal_values(rng, dims, spread, most, pieces=(), kind=jnp.bfloat16):
    result = spread * jax.random.normal(rng, dims, jnp.float32)
    if pieces:
        result = result * block_levels(rng, dims, pieces, -0.22, 0.18)
    return jnp.clip(result, -most, most).astype(kind)


def setup_inputs(seed: int = 0) -> dict:
    key_list = jax.random.split(jax.random.key(seed), 7)
    return {
        "tie_rows": normal_values(key_list[0], (NBLK, ROWS, COLS), ROWS ** -0.5, 0.375, ((0, 4),)),
        "point_counts": draw_point_counts(jax.random.fold_in(key_list[6], 71), 0),
        "pattern": plant((jax.random.randint(key_list[2], (NSC, NBLK), 0, 16) < 1).astype(jnp.int32), jax.random.fold_in(key_list[2], 1), 0, 1),
        "sensitivity": normal_values(key_list[3], (NSC, SPLINE, SPLINE), 0.02, 0.119628906, ((0, 8),)),
        "damping": jnp.clip(jnp.exp(math.log(8.0) - 2.0794415 * jax.random.uniform(key_list[4], (NSC,), jnp.float32) ** block_levels(key_list[4], (NSC,), ((0, 32),), -0.2, 0.2)), 1.0, 8.0),
        "prior": jnp.clip(jnp.exp(jax.random.uniform(key_list[5], (SHARED,), jnp.float32, math.log(0.25), math.log(4.0))), 0.25, 4.0),
    }


highest = lax.Precision.HIGHEST

def block_gram(tie_rows, point_counts):
    row_index = lax.broadcasted_iota(jnp.int32, (tie_rows.shape[0], tie_rows.shape[1]), 1)
    row_valid = (row_index // 2 < point_counts[:, None]).astype(jnp.float32)
    full_rows = tie_rows.astype(jnp.float32)
    masked_rows = full_rows * row_valid[:, :, None]
    return jnp.einsum('brc,brd->bcd', masked_rows, full_rows, precision=highest)

def scene_info(merged, sensitivity, width):
    basis = jnp.eye(width, dtype=jnp.float32)[None] + sensitivity.astype(jnp.float32)
    corner = merged[:, :width, :width]
    side = merged[:, :width, width:]
    tail = merged[:, width:, width:]
    mixed = jnp.einsum('sab,sbc->sac', corner, basis, precision=highest)
    corner_new = jnp.einsum('sba,sbc->sac', basis, mixed, precision=highest)
    side_new = jnp.einsum('sba,sbc->sac', basis, side, precision=highest)
    upper_half = jnp.concatenate([corner_new, side_new], 2)
    lower_half = jnp.concatenate([jnp.transpose(side_new, (0, 2, 1)), tail], 2)
    return jnp.concatenate([upper_half, lower_half], 1)

def factor_scenes(information, damping, width):
    identity = jnp.eye(width, dtype=jnp.float32)
    corner = information[:, :width, :width] + damping[:, None, None] * identity
    chol_lower = jnp.linalg.cholesky(corner)
    cross = jax.scipy.linalg.solve_triangular(chol_lower, information[:, :width, width:], lower=True)
    reduced = information[:, width:, width:] - jnp.einsum('sab,sac->sbc', cross, cross, precision=highest)
    out_rows = jnp.concatenate([jnp.transpose(chol_lower, (0, 2, 1)), cross], 2)
    return (out_rows, jnp.sum(reduced, 0))

def reference(tie_rows, point_counts, pattern, sensitivity, damping, prior):
    block_grams = block_gram(tie_rows, point_counts)
    grams_flat = block_grams.reshape(NBLK, COLS * COLS)

    def group(items):
        group_pattern, group_sens, group_damp = items
        merged = jnp.dot(group_pattern.astype(jnp.float32), grams_flat, precision=highest).reshape(SC_SHARD, COLS, COLS)
        information = scene_info(merged, group_sens, SPLINE)
        return factor_scenes(information, group_damp, SPLINE)
    rows_out, reduced_parts = lax.map(group, (pattern.reshape(N_SCENE, SC_SHARD, NBLK), sensitivity.reshape(N_SCENE, SC_SHARD, SPLINE, SPLINE), damping.reshape(N_SCENE, SC_SHARD)))
    scene_rows = rows_out.reshape(NSC, SPLINE, COLS)
    total = jnp.diag(prior) + jnp.sum(reduced_parts, 0) / NSC
    return (scene_rows, jnp.transpose(jnp.linalg.cholesky(total)))
```

```python
import functools
import math

import jax
import jax.numpy as jnp
from jax import lax
from jax.experimental import pallas as pl
from jax.experimental.pallas import tpu as pltpu
from jax.sharding import PartitionSpec as P

MESH = pl.DeviceIdType.MESH
F32 = jnp.float32
BF16 = jnp.bfloat16
PANEL = 32
LANES = 128
SUB = 8
VMEM = pl.BlockSpec(memory_space=pltpu.VMEM)


def over_rows(a, b):
    return lax.dot_general(a, b, (((0,), (0,)), ((), ())), preferred_element_type=F32)


def gram_kernel(chunk, most, counts, order, active, rows_ref, out_ref, gram_ref):
    step = pl.program_id(0)

    @pl.when(step == 0)
    def _():
        out_ref[...] = jnp.zeros_like(out_ref)

    half = rows_ref.shape[2] // 2
    row_index = lax.broadcasted_iota(jnp.int32, rows_ref.shape[1:], 0)
    for i in range(chunk):
        rows = rows_ref[i]
        valid = jnp.where(row_index < 2 * counts[step * chunk + i], 1.0, 0.0).astype(BF16)
        kept = rows * valid
        top = over_rows(kept[:, :half], rows)
        gram_ref[i, :half] = top[:, :half]
        gram_ref[i, half : 2 * half] = top[:, half:]
        gram_ref[i, 2 * half :] = over_rows(kept[:, half:], rows[:, half:])
    for i in range(chunk):
        block = step * chunk + i

        def add(k, carry, i=i, block=block):
            scene = order[block * most + k]
            out_ref[scene] += gram_ref[i]
            return carry

        lax.fori_loop(0, active[block], add, 0)


def merged_partials(tie_rows, point_counts, pattern):
    blocks, rows, width = tie_rows.shape
    scenes = pattern.shape[0]
    half = width // 2
    chunk = math.gcd(blocks, 8)
    index = jnp.arange(scenes)
    seen = (pattern != 0).astype(jnp.int32).T
    before = jnp.sum(seen[:, None, :] * (index[None, :] < index[:, None])[None], 2)
    hits = (before[:, :, None] == index) & (seen[:, :, None] != 0)
    order = jnp.sum(jnp.where(hits, index[None, :, None], 0), 1).reshape(-1)
    return pl.pallas_call(
        functools.partial(gram_kernel, chunk, scenes),
        grid_spec=pltpu.PrefetchScalarGridSpec(
            num_scalar_prefetch=3,
            grid=(blocks // chunk,),
            in_specs=[pl.BlockSpec((chunk, rows, width), lambda i, *_: (i, 0, 0))],
            out_specs=pl.BlockSpec((scenes, 3 * half, half), lambda i, *_: (0, 0, 0)),
            scratch_shapes=[pltpu.VMEM((chunk, 3 * half, half), F32)],
        ),
        out_shape=jax.ShapeDtypeStruct((scenes, 3 * half, half), F32),
        name="grams",
    )(point_counts, order.astype(jnp.int32), jnp.sum(seen, 1), tie_rows)


def scatter_kernel(n, own, part, out, got, summed, far, s1, r1, s2, r2):
    me = lax.axis_index("tie")
    pairs = n // 2
    parity = lax.rem(me, 2)
    group = me // 2
    partner = me + 1 - 2 * parity

    def member(k, side):
        return lax.rem(group + k, pairs) * 2 + side

    barrier = pltpu.get_barrier_semaphore()
    pl.semaphore_signal(barrier, inc=1, device_id={"tie": partner}, device_id_type=MESH)
    for k in range(1, pairs):
        pl.semaphore_signal(
            barrier, inc=1, device_id={"tie": member(k, parity)}, device_id_type=MESH
        )
    pl.semaphore_wait(barrier, pairs)

    order = [(k, q) for k in list(range(1, pairs)) + [0] for q in range(own)]
    first, second = {}, {}
    for k, q in order:
        slot = k * own + q
        first[k, q] = pltpu.make_async_remote_copy(
            src_ref=part.at[member(k, 1 - parity) * own + q],
            dst_ref=got.at[slot],
            send_sem=s1.at[slot],
            recv_sem=r1.at[slot],
            device_id={"tie": partner},
            device_id_type=MESH,
        )
        first[k, q].start()
    for k, q in order:
        slot = k * own + q
        first[k, q].wait_recv()
        mine = member(k, parity) * own + q
        if k == 0:
            out[q] = part[mine] + got[slot]
        else:
            summed[slot] = part[mine] + got[slot]
            second[k, q] = pltpu.make_async_remote_copy(
                src_ref=summed.at[slot],
                dst_ref=far.at[slot],
                send_sem=s2.at[slot],
                recv_sem=r2.at[slot],
                device_id={"tie": member(k, parity)},
                device_id_type=MESH,
            )
            second[k, q].start()
    for k, q in order:
        if k:
            second[k, q].wait_recv()
            out[q] += far[k * own + q]
    for k, q in order:
        first[k, q].wait_send()
        if k:
            second[k, q].wait_send()


def scatter_sum(partials, n):
    scenes, high, wide = partials.shape
    own = scenes // n
    slots = own * (n // 2)
    block = (slots, high, wide)
    dma = pltpu.SemaphoreType.DMA((slots,))
    return pl.pallas_call(
        functools.partial(scatter_kernel, n, own),
        out_shape=jax.ShapeDtypeStruct((own, high, wide), F32),
        in_specs=[VMEM],
        out_specs=VMEM,
        scratch_shapes=[pltpu.VMEM(block, F32)] * 3 + [dma] * 4,
        compiler_params=pltpu.CompilerParams(collective_id=0, has_side_effects=True),
        name="scatter",
    )(partials)


def two_parts(x):
    high = x.astype(BF16)
    return high, (x - high.astype(F32)).astype(BF16)

def eliminate(panels, first):
    height, wide = panels[0].shape
    tile = (SUB, LANES)
    count = height // SUB
    rows = [[p[SUB * h : SUB * (h + 1)] for h in range(count)] for p in panels]
    row_index = lax.broadcasted_iota(jnp.int32, (SUB, wide), 0)
    lane = lax.broadcasted_iota(jnp.int32, (SUB, wide), 1)
    tile_row = lax.broadcasted_iota(jnp.int32, tile, 0)
    below = [tile_row > k for k in range(SUB)]
    def spread(x):
        return x if wide == LANES else (jnp.concatenate([x] * (wide // LANES), 1) if wide > LANES else x[:, :wide])
    for g in range(count):
        start = first + SUB * g
        cols = [
            [[jnp.broadcast_to(r[h][:, start + m : start + m + 1], tile) for h in range(g, count)] for m in range(SUB)]
            for r in rows
        ]
        for q, r in enumerate(rows):
            b = cols[q]
            pivots = b[0][0]
            for k in range(SUB):
                inverse = 1.0 / b[k][0][k : k + 1]
                pivots = jnp.where(tile_row == k, b[k][0], pivots)
                scaled = r[g][k : k + 1] * spread(inverse)
                factors = [b[m][0][k : k + 1] * inverse for m in range(k + 1, SUB)]
                for h in range(g, count):
                    column = b[k][h - g]
                    if h == g:
                        if k == SUB - 1:
                            continue
                        column = jnp.where(below[k], column, 0.0)
                    for m in range(k + 1, SUB):
                        b[m][h - g] = b[m][h - g] - column * factors[m - k - 1]
                    r[h] = r[h] - spread(column) * scaled
            r[g] = jnp.where(lane >= row_index + start, r[g] * spread(lax.rsqrt(pivots)), 0.0)
    return rows

def factor_kernel(panel, damping, merged, sens, out, reduced, info, spread_sens):
    own, width, _ = info.shape
    spline = out.shape[1]
    half = width // 2
    beyond = width - spline
    for q in range(own):
        wide = jnp.concatenate([sens[q], jnp.zeros((spline, beyond), BF16)], 1)
        spread_sens[q] = jnp.concatenate([wide, jnp.zeros((beyond, width), BF16)], 0)
    row_index = lax.broadcasted_iota(jnp.int32, (width, width), 0)
    lane = lax.broadcasted_iota(jnp.int32, (width, width), 1)
    on_diagonal = (row_index == lane) & (row_index < spline)
    for q in range(own):
        side = merged[q, half : 2 * half]
        top = jnp.concatenate([merged[q, :half], side], 1)
        bottom = jnp.concatenate([side.T, merged[q, 2 * half :]], 1)
        whole = jnp.concatenate([top, bottom], 0)
        s = spread_sens[q]
        mixed = whole + sum(
            jnp.dot(piece, s, preferred_element_type=F32) for piece in two_parts(whole)
        )
        result = mixed + sum(over_rows(s, piece) for piece in two_parts(mixed))
        info[q] = result + jnp.where(on_diagonal, damping[q], 0.0)
    for start in range(0, spline, panel):
        base = start // LANES * LANES
        panels = [info[q, start : start + panel, base:] for q in range(own)]
        rows = eliminate(panels, start - base)
        if base:
            out[:, start : start + panel, :base] = jnp.zeros((own, panel, base), F32)
        after = start + panel
        for q in range(own):
            block = jnp.concatenate(rows[q], 0)
            out[q, start : start + panel, base:] = block
            high, low = two_parts(block)
            left = jnp.concatenate([high, high, low], 0)
            right = jnp.concatenate([high, low, high], 0)
            for top in range(after // LANES * LANES, width, LANES):
                skip = max(after - top, 0)
                update = over_rows(left[:, top - base : top - base + LANES], right[:, top - base :])
                info[q, top + skip : top + LANES, top:] -= update[skip:]
    total = info[0, spline:, half:]
    for q in range(1, own):
        total = total + info[q, spline:, half:]
    total = total[:, spline - half :]
    middle = (width - spline) // 2
    reduced[...] = jnp.concatenate([total[:middle], total[middle:]], 1)

def factor_scenes(merged, sensitivity, damping, width):
    own = damping.shape[0]
    spline = sensitivity.shape[1]
    beyond = width - spline
    mine = lax.dynamic_slice_in_dim(sensitivity, lax.axis_index("tie") * own, own)
    return pl.pallas_call(
        functools.partial(factor_kernel, PANEL),
        in_specs=[pl.BlockSpec(memory_space=pltpu.SMEM), VMEM, VMEM],
        out_specs=[VMEM, VMEM],
        scratch_shapes=[
            pltpu.VMEM((own, width, width), F32),
            pltpu.VMEM((own, width, width), BF16),
        ],
        out_shape=[
            jax.ShapeDtypeStruct((own, spline, width), F32),
            jax.ShapeDtypeStruct((beyond // 2, 2 * beyond), F32),
        ],
        name="factor",
    )(damping, merged, mine)


def total_kernel(axes, x, out, *scratch):
    barrier = pltpu.get_barrier_semaphore()
    for name, n in axes:
        me = lax.axis_index(name)
        for k in range(1, n):
            pl.semaphore_signal(
                barrier, inc=1, device_id={name: lax.rem(me + k, n)}, device_id_type=MESH
            )
    pl.semaphore_wait(barrier, sum(n - 1 for _, n in axes))
    value = x
    for at, (name, n) in enumerate(axes):
        slots, send, recv = scratch[3 * at : 3 * at + 3]
        me = lax.axis_index(name)
        slots[0] = value[...]
        copies = []
        for k in range(1, n):
            copies.append(
                pltpu.make_async_remote_copy(
                    src_ref=slots.at[0],
                    dst_ref=slots.at[k],
                    send_sem=send.at[k],
                    recv_sem=recv.at[k],
                    device_id={name: lax.rem(me + k, n)},
                    device_id_type=MESH,
                )
            )
            copies[-1].start()
        for copy in copies:
            copy.wait_recv()
        acc = slots[me]
        for i in range(1, n):
            acc = acc + slots[lax.rem(me - i + n, n)]
        for copy in copies:
            copy.wait_send()
        out[...] = acc
        value = out


def total_sum(x, axes):
    scratch = []
    for _, n in axes:
        scratch += [pltpu.VMEM((n,) + x.shape, F32)]
        scratch += [pltpu.SemaphoreType.DMA((n,))] * 2
    return pl.pallas_call(
        functools.partial(total_kernel, axes),
        out_shape=jax.ShapeDtypeStruct(x.shape, F32),
        in_specs=[VMEM],
        out_specs=VMEM,
        scratch_shapes=scratch,
        compiler_params=pltpu.CompilerParams(collective_id=1, has_side_effects=True),
        name="total",
    )(x)


def last_kernel(scale, x, prior, out):
    shared = prior.shape[1]
    lane = lax.broadcasted_iota(jnp.int32, (shared, shared), 1)
    row = lax.broadcasted_iota(jnp.int32, (shared, shared), 0)
    packed = x[...]
    value = jnp.concatenate([packed[:, :shared], packed[:, shared:]], 0)
    value = value * scale + jnp.where(lane == row, prior[...], 0.0)
    out[...] = jnp.concatenate(eliminate([value], 0)[0], 0)

def last_factor(x, prior, scale):
    shared = prior.shape[0]
    return pl.pallas_call(
        functools.partial(last_kernel, scale),
        out_shape=jax.ShapeDtypeStruct((shared, shared), F32),
        in_specs=[VMEM, VMEM],
        out_specs=VMEM,
        name="last",
    )(x, prior[None, :])


def on_device(axes, tie_rows, point_counts, pattern, sensitivity, damping, prior):
    sizes = dict(axes)
    width = tie_rows.shape[2]
    partials = merged_partials(tie_rows, point_counts, pattern)
    merged = scatter_sum(partials, sizes["tie"])
    scene_rows, reduced = factor_scenes(merged, sensitivity, damping, width)
    total = total_sum(reduced, axes)
    scenes = damping.shape[0] * math.prod(sizes.values())
    return scene_rows, last_factor(total, prior, 1.0 / scenes)


def solution(mesh):
    axes = (("tie", mesh.shape["tie"]), ("scene", mesh.shape["scene"]))
    placed = (
        P("tie", None, None),
        P("tie"),
        P("scene", "tie"),
        P("scene", None, None),
        P(("scene", "tie")),
        P(),
    )
    return jax.shard_map(
        functools.partial(on_device, axes),
        mesh=mesh,
        in_specs=placed,
        out_specs=(P(("scene", "tie"), None, None), P()),
        check_vma=False,
    )
```

```python
import functools
import math

import jax
import jax.numpy as jnp
from jax import lax
from jax.experimental import pallas as pl
from jax.experimental.pallas import tpu as pltpu
from jax.sharding import PartitionSpec as P


MESH = pl.DeviceIdType.MESH
F32 = jnp.float32
BF16 = jnp.bfloat16
PANEL = 32
LANES = 128
SUB = 8
UNROLL = 8
DEPTH = 32
PIECES = 2
VMEM = pl.BlockSpec(memory_space=pltpu.VMEM)


def over_rows(a, b):
    return lax.dot_general(a, b, (((0,), (0,)), ((), ())), preferred_element_type=F32)


def gram_kernel(groups, own, pairs, counts, pattern, rows, *rest):
    outs = rest[: len(groups)]
    ring, acc, entries, arrived = rest[len(groups) :]
    depth, _, wide = ring.shape
    half = wide // 2
    total = pattern.shape[1]
    stride = 1 << (total - 1).bit_length()
    me = lax.axis_index("tie")

    def fetch(n):
        at = lax.rem(n, depth)
        block = entries[n] & (stride - 1)
        return pltpu.make_async_copy(rows.at[block], ring.at[at], arrived.at[at])

    def start_fetch(n, carry):
        fetch(n).start()
        return carry

    filled = jnp.int32(0)
    place = 0
    for hop, side, offset, size in groups:
        device = lax.rem(me // 2 + hop, pairs) * 2 + lax.rem(me + side, 2)

        def scan(q, n, device=device, offset=offset, place=place):
            scene = device * own + offset + q
            base = (place + q) * stride
            was = n
            for block in range(total):
                entries[n] = base + block
                n = n + pattern[scene, block]
            lax.fori_loop(jnp.minimum(was, depth), jnp.minimum(n, depth), start_fetch, 0)
            return n

        filled = lax.fori_loop(0, size, scan, filled)
        place += size
    acc[...] = jnp.zeros_like(acc)
    reach = lax.broadcasted_iota(jnp.int32, (2 * SUB, wide), 1)

    def step(it, carry):
        for u in range(UNROLL):
            n = it * UNROLL + u

            @pl.when(n < filled)
            def _(n=n):
                fetch(n).wait()

        for u in range(UNROLL):
            n = it * UNROLL + u
            at = jnp.minimum(n, filled - 1)
            entry = entries[at]
            keep = jnp.where(n < filled, 2 * counts[entry & (stride - 1)], 0)
            value = ring[lax.rem(at, depth)]
            mask = jnp.where(reach < keep, 1.0, 0.0).astype(BF16)
            kept = value.T * jnp.concatenate([mask] * (wide // (2 * SUB)), 0)
            top = jnp.dot(kept[:half], value, preferred_element_type=F32)
            bottom = jnp.dot(kept[half:], value[:, half:], preferred_element_type=F32)
            to = entry // stride
            acc[to, :half] += top[:, :half]
            acc[to, half : 2 * half] += top[:, half:]
            acc[to, 2 * half :] += bottom
        for u in range(UNROLL):
            n = it * UNROLL + u + depth

            @pl.when(n < filled)
            def _(n=n):
                fetch(n).start()

        return carry

    lax.fori_loop(0, (filled + UNROLL - 1) // UNROLL, step, 0)
    row = lax.broadcasted_iota(jnp.int32, (half, half), 0)
    lane = lax.broadcasted_iota(jnp.int32, (half, half), 1)
    first = lax.broadcasted_iota(jnp.int32, (SUB, half), 0) == 0
    place = 0
    for out, (_, _, _, size) in zip(outs, groups):
        for q in range(size):
            low = acc[place, 2 * half :]
            out[q, :half] = acc[place, half : 2 * half]
            out[q, half : 2 * half] = jnp.where(row <= lane, acc[place, :half], low)
            diagonal = jnp.sum(jnp.where(row == lane, low, 0.0), 0, keepdims=True)
            out[q, 2 * half :] = jnp.where(first, diagonal, 0.0)
            place += 1


def gram_sums(tie_rows, point_counts, pattern, groups, own, n):
    total, height, wide = tie_rows.shape
    half = wide // 2
    sizes = [group[3] for group in groups]
    most = sum(sizes)
    smem = pl.BlockSpec(memory_space=pltpu.SMEM)
    return pl.pallas_call(
        functools.partial(gram_kernel, groups, own, n // 2),
        in_specs=[smem, smem, pl.BlockSpec(memory_space=pl.ANY)],
        out_specs=[VMEM] * len(sizes),
        out_shape=[jax.ShapeDtypeStruct((size, wide + SUB, half), F32) for size in sizes],
        scratch_shapes=[
            pltpu.VMEM((DEPTH, height, wide), BF16),
            pltpu.VMEM((most, 3 * half, half), F32),
            pltpu.SMEM((most * total + 1,), jnp.int32),
            pltpu.SemaphoreType.DMA((DEPTH,)),
        ],
        compiler_params=pltpu.CompilerParams(vmem_limit_bytes=56 << 20),
    )(point_counts, pattern, tie_rows)


def swap_cores(x, n):
    return lax.ppermute(x, "tie", [(t, t ^ 1) for t in range(n)])


def send_over(x, n, hop):
    pairs = n // 2
    return lax.ppermute(x, "tie", [(t, (t // 2 + hop) % pairs * 2 + t % 2) for t in range(n)])


def merged_sums(tie_rows, point_counts, pattern, own, n):
    size = own // PIECES
    parts = []
    for hop in range(1, n // 2):
        for offset in range(0, own, size):
            groups = [(hop, side, offset, size) for side in (1, 0)]
            theirs, mine = gram_sums(tie_rows, point_counts, pattern, groups, own, n)
            both = mine + swap_cores(theirs, n)
            both, point_counts = lax.optimization_barrier((both, point_counts))
            parts.append((offset, send_over(both, n, hop)))
    groups = [(0, 1, 0, own), (0, 0, 0, own)]
    theirs, mine = gram_sums(tie_rows, point_counts, pattern, groups, own, n)
    return [(0, mine), (0, swap_cores(theirs, n))] + parts


def two_parts(x):
    high = x.astype(BF16)
    return high, (x - high.astype(F32)).astype(BF16)


def eliminate(panels, first):
    height, wide = panels[0].shape
    tile = (SUB, LANES)
    count = height // SUB
    rows = [[p[SUB * h : SUB * (h + 1)] for h in range(count)] for p in panels]
    row_index = lax.broadcasted_iota(jnp.int32, (SUB, wide), 0)
    lane = lax.broadcasted_iota(jnp.int32, (SUB, wide), 1)
    tile_row = lax.broadcasted_iota(jnp.int32, tile, 0)
    below = [tile_row > k for k in range(SUB)]

    def spread(x):
        return x if wide == LANES else (jnp.concatenate([x] * (wide // LANES), 1) if wide > LANES else x[:, :wide])

    for g in range(count):
        start = first + SUB * g
        cols = [
            [[jnp.broadcast_to(r[h][:, start + m : start + m + 1], tile) for h in range(g, count)] for m in range(SUB)]
            for r in rows
        ]
        for q, r in enumerate(rows):
            b = cols[q]
            pivots = b[0][0]
            for k in range(SUB):
                inverse = 1.0 / b[k][0][k : k + 1]
                pivots = jnp.where(tile_row == k, b[k][0], pivots)
                scaled = r[g][k : k + 1] * spread(inverse)
                factors = [b[m][0][k : k + 1] * inverse for m in range(k + 1, SUB)]
                for h in range(g, count):
                    column = b[k][h - g]
                    if h == g:
                        if k == SUB - 1:
                            continue
                        column = jnp.where(below[k], column, 0.0)
                    for m in range(k + 1, SUB):
                        b[m][h - g] = b[m][h - g] - column * factors[m - k - 1]
                    r[h] = r[h] - spread(column) * scaled
            r[g] = jnp.where(lane >= row_index + start, r[g] * spread(lax.rsqrt(pivots)), 0.0)
    return rows


def factor_kernel(panel, offsets, damping, sens, *rest):
    parts = rest[: len(offsets)]
    out, reduced, info, spread_sens = rest[len(offsets) :]
    own, width, _ = info.shape
    spline = out.shape[1]
    half = width // 2
    beyond = width - spline
    for q in range(own):
        wide = jnp.concatenate([sens[q], jnp.zeros((spline, beyond), BF16)], 1)
        spread_sens[q] = jnp.concatenate([wide, jnp.zeros((beyond, width), BF16)], 0)
    row_index = lax.broadcasted_iota(jnp.int32, (width, width), 0)
    lane = lax.broadcasted_iota(jnp.int32, (width, width), 1)
    on_diagonal = (row_index == lane) & (row_index < spline)
    across = lane[:half, :half] - row_index[:half, :half]
    for q in range(own):
        packed = sum(
            part[q - offset]
            for offset, part in zip(offsets, parts)
            if offset <= q < offset + part.shape[0]
        )
        side, both = packed[:half], packed[half : 2 * half]
        upper = jnp.where(across > 0, both, 0.0)
        first = jnp.where(across >= 0, both, upper.T)
        lower = jnp.where(across < 0, both, 0.0)
        last = lower + jnp.where(across == 0, packed[2 * half : 2 * half + 1], lower.T)
        top = jnp.concatenate([first, side], 1)
        bottom = jnp.concatenate([side.T, last], 1)
        whole = jnp.concatenate([top, bottom], 0)
        s = spread_sens[q]
        mixed = whole + sum(
            jnp.dot(piece, s, preferred_element_type=F32) for piece in two_parts(whole)
        )
        result = mixed + sum(over_rows(s, piece) for piece in two_parts(mixed))
        info[q] = result + jnp.where(on_diagonal, damping[q], 0.0)
    for start in range(0, spline, panel):
        base = start // LANES * LANES
        panels = [info[q, start : start + panel, base:] for q in range(own)]
        rows = eliminate(panels, start - base)
        if base:
            out[:, start : start + panel, :base] = jnp.zeros((own, panel, base), F32)
        after = start + panel
        for q in range(own):
            block = jnp.concatenate(rows[q], 0)
            out[q, start : start + panel, base:] = block
            high, low = two_parts(block)
            left = jnp.concatenate([high, high, low], 0)
            right = jnp.concatenate([high, low, high], 0)
            for top in range(after // LANES * LANES, width, LANES):
                skip = max(after - top, 0)
                update = over_rows(left[:, top - base : top - base + LANES], right[:, top - base :])
                info[q, top + skip : top + LANES, top:] -= update[skip:]
    total = info[0, spline:, half:]
    for q in range(1, own):
        total = total + info[q, spline:, half:]
    total = total[:, spline - half :]
    middle = (width - spline) // 2
    reduced[...] = jnp.concatenate([total[:middle], total[middle:]], 1)


def factor_scenes(parts, sensitivity, damping, width):
    own = damping.shape[0]
    spline = sensitivity.shape[1]
    beyond = width - spline
    mine = lax.dynamic_slice_in_dim(sensitivity, lax.axis_index("tie") * own, own)
    offsets = [offset for offset, _ in parts]
    return pl.pallas_call(
        functools.partial(factor_kernel, PANEL, offsets),
        in_specs=[pl.BlockSpec(memory_space=pltpu.SMEM)] + [VMEM] * (1 + len(parts)),
        out_specs=[VMEM, VMEM],
        scratch_shapes=[
            pltpu.VMEM((own, width, width), F32),
            pltpu.VMEM((own, width, width), BF16),
        ],
        out_shape=[
            jax.ShapeDtypeStruct((own, spline, width), F32),
            jax.ShapeDtypeStruct((beyond // 2, 2 * beyond), F32),
        ],
        compiler_params=pltpu.CompilerParams(vmem_limit_bytes=32 << 20),
        name="factor",
    )(damping, mine, *(part for _, part in parts))


def total_kernel(axes, x, out, *scratch):
    barrier = pltpu.get_barrier_semaphore()
    for name, n in axes:
        me = lax.axis_index(name)
        for k in range(1, n):
            pl.semaphore_signal(
                barrier, inc=1, device_id={name: lax.rem(me + k, n)}, device_id_type=MESH
            )
    pl.semaphore_wait(barrier, sum(n - 1 for _, n in axes))
    value = x
    for at, (name, n) in enumerate(axes):
        slots, send, recv = scratch[3 * at : 3 * at + 3]
        me = lax.axis_index(name)
        slots[0] = value[...]
        copies = []
        for k in range(1, n):
            copies.append(
                pltpu.make_async_remote_copy(
                    src_ref=slots.at[0],
                    dst_ref=slots.at[k],
                    send_sem=send.at[k],
                    recv_sem=recv.at[k],
                    device_id={name: lax.rem(me + k, n)},
                    device_id_type=MESH,
                )
            )
            copies[-1].start()
        for copy in copies:
            copy.wait_recv()
        acc = slots[me]
        for i in range(1, n):
            acc = acc + slots[lax.rem(me - i + n, n)]
        for copy in copies:
            copy.wait_send()
        out[...] = acc
        value = out


def total_sum(x, axes):
    scratch = []
    for _, n in axes:
        scratch += [pltpu.VMEM((n,) + x.shape, F32)]
        scratch += [pltpu.SemaphoreType.DMA((n,))] * 2
    return pl.pallas_call(
        functools.partial(total_kernel, axes),
        out_shape=jax.ShapeDtypeStruct(x.shape, F32),
        in_specs=[VMEM],
        out_specs=VMEM,
        scratch_shapes=scratch,
        compiler_params=pltpu.CompilerParams(collective_id=1, has_side_effects=True),
        name="total",
    )(x)


def last_kernel(scale, x, prior, out):
    shared = prior.shape[1]
    lane = lax.broadcasted_iota(jnp.int32, (shared, shared), 1)
    row = lax.broadcasted_iota(jnp.int32, (shared, shared), 0)
    packed = x[...]
    value = jnp.concatenate([packed[:, :shared], packed[:, shared:]], 0)
    value = value * scale + jnp.where(lane == row, prior[...], 0.0)
    out[...] = jnp.concatenate(eliminate([value], 0)[0], 0)


def last_factor(x, prior, scale):
    shared = prior.shape[0]
    return pl.pallas_call(
        functools.partial(last_kernel, scale),
        out_shape=jax.ShapeDtypeStruct((shared, shared), F32),
        in_specs=[VMEM, VMEM],
        out_specs=VMEM,
        name="last",
    )(x, prior[None, :])


def on_device(axes, tie_rows, point_counts, pattern, sensitivity, damping, prior):
    sizes = dict(axes)
    own = damping.shape[0]
    width = tie_rows.shape[2]
    parts = merged_sums(tie_rows, point_counts, pattern, own, sizes["tie"])
    scene_rows, reduced = factor_scenes(parts, sensitivity, damping, width)
    total = total_sum(reduced, axes)
    scenes = own * math.prod(sizes.values())
    return scene_rows, last_factor(total, prior, 1.0 / scenes)


def solution(mesh):
    axes = (("tie", mesh.shape["tie"]), ("scene", mesh.shape["scene"]))
    placed = (
        P("tie", None, None),
        P("tie"),
        P("scene", "tie"),
        P("scene", None, None),
        P(("scene", "tie")),
        P(),
    )
    return jax.shard_map(
        functools.partial(on_device, axes),
        mesh=mesh,
        in_specs=placed,
        out_specs=(P(("scene", "tie"), None, None), P()),
        check_vma=False,
    )
```

```python
import functools

import jax
import jax.numpy as jnp
from jax import lax
from jax.experimental import pallas as pl
from jax.experimental.pallas import tpu as pltpu
from jax.sharding import PartitionSpec as P


MESH = pl.DeviceIdType.MESH
F32 = jnp.float32
BF16 = jnp.bfloat16
PANEL = 32
LANES = 128
SUB = 8
UNROLL = 8
DEPTH = 32
PIECES = 1
VMEM = pl.BlockSpec(memory_space=pltpu.VMEM)


def over_rows(a, b):
    return lax.dot_general(a, b, (((0,), (0,)), ((), ())), preferred_element_type=F32)


def gram_kernel(groups, own, pairs, counts, pattern, rows, *rest):
    outs = rest[: len(groups)]
    ring, acc, entries, arrived = rest[len(groups) :]
    depth, _, wide = ring.shape
    half = wide // 2
    total = pattern.shape[1]
    stride = 1 << (total - 1).bit_length()
    me = lax.axis_index("tie")

    def fetch(n):
        at = lax.rem(n, depth)
        block = entries[n] & (stride - 1)
        return pltpu.make_async_copy(rows.at[block], ring.at[at], arrived.at[at])

    def start_fetch(n, carry):
        fetch(n).start()
        return carry

    filled = jnp.int32(0)
    place = 0
    for hop, side, offset, size in groups:
        device = lax.rem(me // 2 + hop, pairs) * 2 + lax.rem(me + side, 2)

        def scan(q, n, device=device, offset=offset, place=place):
            scene = device * own + offset + q
            base = (place + q) * stride
            was = n
            for block in range(total):
                entries[n] = base + block
                n = n + pattern[scene, block]
            lax.fori_loop(jnp.minimum(was, depth), jnp.minimum(n, depth), start_fetch, 0)
            return n

        filled = lax.fori_loop(0, size, scan, filled)
        place += size
    acc[...] = jnp.zeros_like(acc)
    reach = lax.broadcasted_iota(jnp.int32, (2 * SUB, wide), 1)

    def step(it, carry):
        for u in range(UNROLL):
            n = it * UNROLL + u

            @pl.when(n < filled)
            def _(n=n):
                fetch(n).wait()

        for u in range(UNROLL):
            n = it * UNROLL + u
            at = jnp.minimum(n, filled - 1)
            entry = entries[at]
            keep = jnp.where(n < filled, 2 * counts[entry & (stride - 1)], 0)
            value = ring[lax.rem(at, depth)]
            mask = jnp.where(reach < keep, 1.0, 0.0).astype(BF16)
            kept = value.T * jnp.concatenate([mask] * (wide // (2 * SUB)), 0)
            top = jnp.dot(kept[:half], value, preferred_element_type=F32)
            bottom = jnp.dot(kept[half:], value[:, half:], preferred_element_type=F32)
            to = entry // stride
            acc[to, :half] += top[:, :half]
            acc[to, half : 2 * half] += top[:, half:]
            acc[to, 2 * half :] += bottom
        for u in range(UNROLL):
            n = it * UNROLL + u + depth

            @pl.when(n < filled)
            def _(n=n):
                fetch(n).start()

        return carry

    lax.fori_loop(0, (filled + UNROLL - 1) // UNROLL, step, 0)
    row = lax.broadcasted_iota(jnp.int32, (half, half), 0)
    lane = lax.broadcasted_iota(jnp.int32, (half, half), 1)
    first = lax.broadcasted_iota(jnp.int32, (SUB, half), 0) == 0
    place = 0
    for out, (_, _, _, size) in zip(outs, groups):
        for q in range(size):
            low = acc[place, 2 * half :]
            out[q, :half] = acc[place, half : 2 * half]
            out[q, half : 2 * half] = jnp.where(row <= lane, acc[place, :half], low)
            diagonal = jnp.sum(jnp.where(row == lane, low, 0.0), 0, keepdims=True)
            out[q, 2 * half :] = jnp.where(first, diagonal, 0.0)
            place += 1


def gram_sums(tie_rows, point_counts, pattern, groups, own, n):
    total, height, wide = tie_rows.shape
    half = wide // 2
    sizes = [group[3] for group in groups]
    most = sum(sizes)
    smem = pl.BlockSpec(memory_space=pltpu.SMEM)
    return pl.pallas_call(
        functools.partial(gram_kernel, groups, own, n // 2),
        in_specs=[smem, smem, pl.BlockSpec(memory_space=pl.ANY)],
        out_specs=[VMEM] * len(sizes),
        out_shape=[jax.ShapeDtypeStruct((size, wide + SUB, half), F32) for size in sizes],
        scratch_shapes=[
            pltpu.VMEM((DEPTH, height, wide), BF16),
            pltpu.VMEM((most, 3 * half, half), F32),
            pltpu.SMEM((most * total + 1,), jnp.int32),
            pltpu.SemaphoreType.DMA((DEPTH,)),
        ],
        compiler_params=pltpu.CompilerParams(vmem_limit_bytes=50 << 20),
    )(point_counts, pattern, tie_rows)


def swap_cores(x, n):
    return lax.ppermute(x, "tie", [(t, t ^ 1) for t in range(n)])


def send_over(x, n, hop):
    pairs = n // 2
    return lax.ppermute(x, "tie", [(t, (t // 2 + hop) % pairs * 2 + t % 2) for t in range(n)])


def merged_sums(tie_rows, point_counts, pattern, own, n):
    size = own // PIECES
    parts = []
    for hop in range(1, n // 2):
        for offset in range(0, own, size):
            groups = [(hop, side, offset, size) for side in (1, 0)]
            theirs, mine = gram_sums(tie_rows, point_counts, pattern, groups, own, n)
            both = mine + swap_cores(theirs, n)
            both, point_counts = lax.optimization_barrier((both, point_counts))
            parts.append((offset, send_over(both, n, hop)))
    groups = [(0, 1, 0, own), (0, 0, 0, own)]
    theirs, mine = gram_sums(tie_rows, point_counts, pattern, groups, own, n)
    return [(0, mine), (0, swap_cores(theirs, n))] + parts


def two_parts(x):
    high = x.astype(BF16)
    return high, (x - high.astype(F32)).astype(BF16)


def eliminate(panels, first):
    height, wide = panels[0].shape
    tile = (SUB, LANES)
    count = height // SUB
    rows = [[p[SUB * h : SUB * (h + 1)] for h in range(count)] for p in panels]
    row_index = lax.broadcasted_iota(jnp.int32, (SUB, wide), 0)
    lane = lax.broadcasted_iota(jnp.int32, (SUB, wide), 1)
    tile_row = lax.broadcasted_iota(jnp.int32, tile, 0)
    below = [tile_row > k for k in range(SUB)]

    def spread(x):
        return x if wide == LANES else (jnp.concatenate([x] * (wide // LANES), 1) if wide > LANES else x[:, :wide])

    for g in range(count):
        start = first + SUB * g
        cols = [
            [[jnp.broadcast_to(r[h][:, start + m : start + m + 1], tile) for h in range(g, count)] for m in range(SUB)]
            for r in rows
        ]
        for q, r in enumerate(rows):
            b = cols[q]
            pivots = b[0][0]
            for k in range(SUB):
                inverse = 1.0 / b[k][0][k : k + 1]
                pivots = jnp.where(tile_row == k, b[k][0], pivots)
                scaled = r[g][k : k + 1] * spread(inverse)
                factors = [b[m][0][k : k + 1] * inverse for m in range(k + 1, SUB)]
                for h in range(g, count):
                    column = b[k][h - g]
                    if h == g:
                        if k == SUB - 1:
                            continue
                        column = jnp.where(below[k], column, 0.0)
                    for m in range(k + 1, SUB):
                        b[m][h - g] = b[m][h - g] - column * factors[m - k - 1]
                    r[h] = r[h] - spread(column) * scaled
            r[g] = jnp.where(lane >= row_index + start, r[g] * spread(lax.rsqrt(pivots)), 0.0)
    return rows


def exchange(ref, slots, send, recv, name, n, width=None):
    me = lax.axis_index(name)
    copies = []
    for k in range(1, n):
        other = lax.rem(me + k, n)
        part = ref if width is None else ref.at[pl.ds(pl.multiple_of(other * width, width), width)]
        copies.append(
            pltpu.make_async_remote_copy(
                src_ref=part,
                dst_ref=slots.at[k],
                send_sem=send.at[k],
                recv_sem=recv.at[k],
                device_id={name: other},
                device_id_type=MESH,
            )
        )
        copies[-1].start()
    return copies


def added(slots, name, n):
    me = lax.axis_index(name)
    acc = slots[me]
    for i in range(1, n):
        acc = acc + slots[lax.rem(me - i + n, n)]
    return acc


def finish_kernel(panel, offsets, axes, scale, damping, sens, prior, *rest):
    parts = rest[: len(offsets)]
    scene_rows, factor, info, spread_sens, out = rest[len(offsets) : len(offsets) + 5]
    mine, near, wide_slots, whole, written, s1, r1, s2, r2, s3, r3 = rest[len(offsets) + 5 :]
    barrier = pltpu.get_barrier_semaphore()
    for name, n in axes:
        me = lax.axis_index(name)
        for k in range(1, n):
            pl.semaphore_signal(
                barrier, inc=1, device_id={name: lax.rem(me + k, n)}, device_id_type=MESH
            )
    mine[...] = factor_scenes(panel, offsets, damping, sens, parts, out, info, spread_sens)
    rows = pltpu.make_async_copy(out, scene_rows, written)
    rows.start()
    pl.semaphore_wait(barrier, sum(n - 1 for _, n in axes))
    (tie, n), (scene, groups) = axes
    chunk = mine.shape[0] // n
    me = lax.axis_index(tie)
    own = pl.ds(pl.multiple_of(me * chunk, chunk), chunk)
    near[0] = mine[own]
    first = exchange(mine, near, s1, r1, tie, n, chunk)
    for copy in first:
        copy.wait_recv()
    wide_slots[0] = added(near, tie, n)
    second = exchange(wide_slots.at[0], wide_slots, s2, r2, scene, groups)
    for copy in second:
        copy.wait_recv()
    whole[own] = added(wide_slots, scene, groups)
    third = []
    for k in range(1, n):
        third.append(
            pltpu.make_async_remote_copy(
                src_ref=whole.at[own],
                dst_ref=whole.at[own],
                send_sem=s3.at[k],
                recv_sem=r3.at[k],
                device_id={tie: lax.rem(me + k, n)},
                device_id_type=MESH,
            )
        )
        third[-1].start()
    for copy in third:
        copy.wait_recv()
    shared = factor.shape[0]
    lane = lax.broadcasted_iota(jnp.int32, (shared, shared), 1)
    row = lax.broadcasted_iota(jnp.int32, (shared, shared), 0)
    value = jnp.concatenate([whole[:, :shared], whole[:, shared:]], 0)
    value = value * scale + jnp.where(lane == row, prior[...], 0.0)
    factor[...] = jnp.concatenate(eliminate([value], 0)[0], 0)
    for copy in first + second + third:
        copy.wait_send()
    rows.wait()


def factor_scenes(panel, offsets, damping, sens, parts, out, info, spread_sens):
    own, width, _ = info.shape
    spline = out.shape[1]
    half = width // 2
    beyond = width - spline
    for q in range(own):
        wide = jnp.concatenate([sens[q], jnp.zeros((spline, beyond), BF16)], 1)
        spread_sens[q] = jnp.concatenate([wide, jnp.zeros((beyond, width), BF16)], 0)
    row_index = lax.broadcasted_iota(jnp.int32, (width, width), 0)
    lane = lax.broadcasted_iota(jnp.int32, (width, width), 1)
    on_diagonal = (row_index == lane) & (row_index < spline)
    across = lane[:half, :half] - row_index[:half, :half]
    for q in range(own):
        packed = sum(
            part[q - offset]
            for offset, part in zip(offsets, parts)
            if offset <= q < offset + part.shape[0]
        )
        side, both = packed[:half], packed[half : 2 * half]
        upper = jnp.where(across > 0, both, 0.0)
        first = jnp.where(across >= 0, both, upper.T)
        lower = jnp.where(across < 0, both, 0.0)
        last = lower + jnp.where(across == 0, packed[2 * half : 2 * half + 1], lower.T)
        top = jnp.concatenate([first, side], 1)
        bottom = jnp.concatenate([side.T, last], 1)
        whole = jnp.concatenate([top, bottom], 0)
        s = spread_sens[q]
        mixed = whole + sum(
            jnp.dot(piece, s, preferred_element_type=F32) for piece in two_parts(whole)
        )
        result = mixed + sum(over_rows(s, piece) for piece in two_parts(mixed))
        info[q] = result + jnp.where(on_diagonal, damping[q], 0.0)
    for start in range(0, spline, panel):
        base = start // LANES * LANES
        panels = [info[q, start : start + panel, base:] for q in range(own)]
        rows = eliminate(panels, start - base)
        if base:
            out[:, start : start + panel, :base] = jnp.zeros((own, panel, base), F32)
        after = start + panel
        for q in range(own):
            block = jnp.concatenate(rows[q], 0)
            out[q, start : start + panel, base:] = block
            high, low = two_parts(block)
            left = jnp.concatenate([high, high, low], 0)
            right = jnp.concatenate([high, low, high], 0)
            for top in range(after // LANES * LANES, width, LANES):
                skip = max(after - top, 0)
                update = over_rows(left[:, top - base : top - base + LANES], right[:, top - base :])
                info[q, top + skip : top + LANES, top:] -= update[skip:]
    total = info[0, spline:, half:]
    for q in range(1, own):
        total = total + info[q, spline:, half:]
    total = total[:, spline - half :]
    middle = (width - spline) // 2
    return jnp.concatenate([total[:middle], total[middle:]], 1)


def finish(parts, sensitivity, damping, prior, width, axes):
    own = damping.shape[0]
    spline = sensitivity.shape[1]
    beyond = width - spline
    (_, n), (_, groups) = axes
    mine = lax.dynamic_slice_in_dim(sensitivity, lax.axis_index("tie") * own, own)
    offsets = [offset for offset, _ in parts]
    scale = 1.0 / (own * n * groups)
    block = (beyond // 2 // n, 2 * beyond)
    dma = pltpu.SemaphoreType.DMA
    return pl.pallas_call(
        functools.partial(finish_kernel, PANEL, offsets, axes, scale),
        in_specs=[pl.BlockSpec(memory_space=pltpu.SMEM)] + [VMEM] * (2 + len(parts)),
        out_specs=[pl.BlockSpec(memory_space=pl.ANY), VMEM],
        scratch_shapes=[
            pltpu.VMEM((own, width, width), F32),
            pltpu.VMEM((own, width, width), BF16),
            pltpu.VMEM((own, spline, width), F32),
            pltpu.VMEM((beyond // 2, 2 * beyond), F32),
            pltpu.VMEM((n,) + block, F32),
            pltpu.VMEM((groups,) + block, F32),
            pltpu.VMEM((beyond // 2, 2 * beyond), F32),
            dma,
            dma((n,)),
            dma((n,)),
            dma((groups,)),
            dma((groups,)),
            dma((n,)),
            dma((n,)),
        ],
        out_shape=[
            jax.ShapeDtypeStruct((own, spline, width), F32),
            jax.ShapeDtypeStruct((beyond, beyond), F32),
        ],
        compiler_params=pltpu.CompilerParams(
            collective_id=0, has_side_effects=True, vmem_limit_bytes=32 << 20
        ),
        name="finish",
    )(damping, mine, prior[None, :], *(part for _, part in parts))


def on_device(axes, tie_rows, point_counts, pattern, sensitivity, damping, prior):
    sizes = dict(axes)
    own = damping.shape[0]
    width = tie_rows.shape[2]
    parts = merged_sums(tie_rows, point_counts, pattern, own, sizes["tie"])
    return finish(parts, sensitivity, damping, prior, width, axes)


def solution(mesh):
    axes = (("tie", mesh.shape["tie"]), ("scene", mesh.shape["scene"]))
    placed = (
        P("tie", None, None),
        P("tie"),
        P("scene", "tie"),
        P("scene", None, None),
        P(("scene", "tie")),
        P(),
    )
    return jax.shard_map(
        functools.partial(on_device, axes),
        mesh=mesh,
        in_specs=placed,
        out_specs=(P(("scene", "tie"), None, None), P()),
        check_vma=False,
    )
```

```python
import functools

import jax
import jax.numpy as jnp
from jax import lax
from jax.experimental import pallas as pl
from jax.experimental.pallas import tpu as pltpu
from jax.sharding import PartitionSpec as P


MESH = pl.DeviceIdType.MESH
F32 = jnp.float32
BF16 = jnp.bfloat16
PANEL = 32
LANES = 128
SUB = 8
UNROLL = 8
DEPTH = 32
PIECES = 1
VMEM = pl.BlockSpec(memory_space=pltpu.VMEM)


def over_rows(a, b):
    return lax.dot_general(a, b, (((0,), (0,)), ((), ())), preferred_element_type=F32)


def gram_kernel(groups, own, pairs, counts, pattern, rows, *rest):
    outs = rest[: len(groups)]
    ring, acc, entries, arrived = rest[len(groups) :]
    depth, _, wide = ring.shape
    half = wide // 2
    total = pattern.shape[1]
    stride = 1 << (total - 1).bit_length()
    me = lax.axis_index("tie")

    def fetch(n):
        at = lax.rem(n, depth)
        block = entries[n] & (stride - 1)
        return pltpu.make_async_copy(rows.at[block], ring.at[at], arrived.at[at])

    def start_fetch(n, carry):
        fetch(n).start()
        return carry

    filled = jnp.int32(0)
    place = 0
    for hop, side, offset, size in groups:
        device = lax.rem(me // 2 + hop, pairs) * 2 + lax.rem(me + side, 2)

        def scan(q, n, device=device, offset=offset, place=place):
            scene = device * own + offset + q
            base = (place + q) * stride
            was = n
            for block in range(total):
                entries[n] = base + block
                n = n + pattern[scene, block]
            lax.fori_loop(jnp.minimum(was, depth), jnp.minimum(n, depth), start_fetch, 0)
            return n

        filled = lax.fori_loop(0, size, scan, filled)
        place += size
    acc[...] = jnp.zeros_like(acc)
    reach = lax.broadcasted_iota(jnp.int32, (2 * SUB, wide), 1)

    def step(it, carry):
        for u in range(UNROLL):
            n = it * UNROLL + u

            @pl.when(n < filled)
            def _(n=n):
                fetch(n).wait()

        for u in range(UNROLL):
            n = it * UNROLL + u
            at = jnp.minimum(n, filled - 1)
            entry = entries[at]
            keep = jnp.where(n < filled, 2 * counts[entry & (stride - 1)], 0)
            value = ring[lax.rem(at, depth)]
            mask = jnp.where(reach < keep, 1.0, 0.0).astype(BF16)
            kept = value.T * jnp.concatenate([mask] * (wide // (2 * SUB)), 0)
            top = jnp.dot(kept[:half], value, preferred_element_type=F32)
            bottom = jnp.dot(kept[half:], value[:, half:], preferred_element_type=F32)
            to = entry // stride
            acc[to, :half] += top[:, :half]
            acc[to, half : 2 * half] += top[:, half:]
            acc[to, 2 * half :] += bottom
        for u in range(UNROLL):
            n = it * UNROLL + u + depth

            @pl.when(n < filled)
            def _(n=n):
                fetch(n).start()

        return carry

    lax.fori_loop(0, (filled + UNROLL - 1) // UNROLL, step, 0)
    row = lax.broadcasted_iota(jnp.int32, (half, half), 0)
    lane = lax.broadcasted_iota(jnp.int32, (half, half), 1)
    first = lax.broadcasted_iota(jnp.int32, (SUB, half), 0) == 0
    place = 0
    for out, (_, _, _, size) in zip(outs, groups):
        for q in range(size):
            low = acc[place, 2 * half :]
            out[q, :half] = acc[place, half : 2 * half]
            out[q, half : 2 * half] = jnp.where(row <= lane, acc[place, :half], low)
            diagonal = jnp.sum(jnp.where(row == lane, low, 0.0), 0, keepdims=True)
            out[q, 2 * half :] = jnp.where(first, diagonal, 0.0)
            place += 1


def gram_sums(tie_rows, point_counts, pattern, groups, own, n):
    total, height, wide = tie_rows.shape
    half = wide // 2
    sizes = [group[3] for group in groups]
    most = sum(sizes)
    smem = pl.BlockSpec(memory_space=pltpu.SMEM)
    return pl.pallas_call(
        functools.partial(gram_kernel, groups, own, n // 2),
        in_specs=[smem, smem, pl.BlockSpec(memory_space=pl.ANY)],
        out_specs=[VMEM] * len(sizes),
        out_shape=[jax.ShapeDtypeStruct((size, wide + SUB, half), F32) for size in sizes],
        scratch_shapes=[
            pltpu.VMEM((DEPTH, height, wide), BF16),
            pltpu.VMEM((most, 3 * half, half), F32),
            pltpu.SMEM((most * total + 1,), jnp.int32),
            pltpu.SemaphoreType.DMA((DEPTH,)),
        ],
        compiler_params=pltpu.CompilerParams(vmem_limit_bytes=16 << 20),
    )(point_counts, pattern, tie_rows)


def swap_cores(x, n):
    return lax.ppermute(x, "tie", [(t, t ^ 1) for t in range(n)])


def send_over(x, n, hop):
    pairs = n // 2
    return lax.ppermute(x, "tie", [(t, (t // 2 + hop) % pairs * 2 + t % 2) for t in range(n)])


def merged_sums(tie_rows, point_counts, pattern, own, n):
    size = own // PIECES
    parts = []
    tie_rows, point_counts, pattern = (
        pltpu.with_memory_space_constraint(x, pltpu.HBM) for x in (tie_rows, point_counts, pattern)
    )
    for hop in range(1, n // 2):
        for offset in range(0, own, size):
            groups = [(hop, side, offset, size) for side in (1, 0)]
            theirs, mine = gram_sums(tie_rows, point_counts, pattern, groups, own, n)
            both = mine + swap_cores(theirs, n)
            both, point_counts = lax.optimization_barrier((both, point_counts))
            parts.append((offset, send_over(both, n, hop)))
    groups = [(0, 1, 0, own), (0, 0, 0, own)]
    theirs, mine = gram_sums(tie_rows, point_counts, pattern, groups, own, n)
    return [(0, mine), (0, swap_cores(theirs, n))] + parts


def two_parts(x):
    high = x.astype(BF16)
    return high, (x - high.astype(F32)).astype(BF16)


def eliminate(panels, first):
    height, wide = panels[0].shape
    tile = (SUB, LANES)
    count = height // SUB
    rows = [[p[SUB * h : SUB * (h + 1)] for h in range(count)] for p in panels]
    row_index = lax.broadcasted_iota(jnp.int32, (SUB, wide), 0)
    lane = lax.broadcasted_iota(jnp.int32, (SUB, wide), 1)
    tile_row = lax.broadcasted_iota(jnp.int32, tile, 0)
    below = [tile_row > k for k in range(SUB)]

    def spread(x):
        return x if wide == LANES else (jnp.concatenate([x] * (wide // LANES), 1) if wide > LANES else x[:, :wide])

    for g in range(count):
        start = first + SUB * g
        cols = [
            [[jnp.broadcast_to(r[h][:, start + m : start + m + 1], tile) for h in range(g, count)] for m in range(SUB)]
            for r in rows
        ]
        for q, r in enumerate(rows):
            b = cols[q]
            pivots = b[0][0]
            for k in range(SUB):
                pivot = jnp.broadcast_to(b[k][0][k : k + 1], tile)
                inverse = 1.0 / pivot
                pivots = jnp.where(tile_row == k, pivot, pivots)
                row = jnp.broadcast_to(r[g][k : k + 1], (SUB, wide))
                ahead = [jnp.broadcast_to(b[m][0][k : k + 1], tile) for m in range(k + 1, SUB)]
                for h in range(g, count):
                    column = b[k][h - g] * inverse
                    if h == g:
                        if k == SUB - 1:
                            continue
                        column = jnp.where(below[k], column, 0.0)
                    for m in range(k + 1, SUB):
                        b[m][h - g] = b[m][h - g] - column * ahead[m - k - 1]
                    r[h] = r[h] - spread(column) * row
            r[g] = jnp.where(lane >= row_index + start, r[g] * spread(lax.rsqrt(pivots)), 0.0)
    return rows


def exchange(ref, slots, send, recv, name, n, width=None):
    me = lax.axis_index(name)
    copies = []
    for k in range(1, n):
        other = lax.rem(me + k, n)
        part = ref if width is None else ref.at[pl.ds(pl.multiple_of(other * width, width), width)]
        copies.append(
            pltpu.make_async_remote_copy(
                src_ref=part,
                dst_ref=slots.at[k],
                send_sem=send.at[k],
                recv_sem=recv.at[k],
                device_id={name: other},
                device_id_type=MESH,
            )
        )
        copies[-1].start()
    return copies


def added(slots, name, n):
    me = lax.axis_index(name)
    acc = slots[me]
    for i in range(1, n):
        acc = acc + slots[lax.rem(me - i + n, n)]
    return acc


def finish_kernel(panel, offsets, axes, scale, damping, sens, prior, *rest):
    parts = rest[: len(offsets)]
    scene_rows, factor, info, spread_sens, out = rest[len(offsets) : len(offsets) + 5]
    mine, near, wide_slots, whole, written, s1, r1, s2, r2, s3, r3 = rest[len(offsets) + 5 :]
    barrier = pltpu.get_barrier_semaphore()
    for name, n in axes:
        me = lax.axis_index(name)
        for k in range(1, n):
            pl.semaphore_signal(
                barrier, inc=1, device_id={name: lax.rem(me + k, n)}, device_id_type=MESH
            )
    mine[...] = factor_scenes(panel, offsets, damping, sens, parts, out, info, spread_sens)
    rows = pltpu.make_async_copy(out, scene_rows, written)
    rows.start()
    pl.semaphore_wait(barrier, sum(n - 1 for _, n in axes))
    (tie, n), (scene, groups) = axes
    chunk = mine.shape[0] // n
    me = lax.axis_index(tie)
    own = pl.ds(pl.multiple_of(me * chunk, chunk), chunk)
    near[0] = mine[own]
    first = exchange(mine, near, s1, r1, tie, n, chunk)
    for copy in first:
        copy.wait_recv()
    wide_slots[0] = added(near, tie, n)
    second = exchange(wide_slots.at[0], wide_slots, s2, r2, scene, groups)
    for copy in second:
        copy.wait_recv()
    whole[own] = added(wide_slots, scene, groups)
    third = []
    for k in range(1, n):
        third.append(
            pltpu.make_async_remote_copy(
                src_ref=whole.at[own],
                dst_ref=whole.at[own],
                send_sem=s3.at[k],
                recv_sem=r3.at[k],
                device_id={tie: lax.rem(me + k, n)},
                device_id_type=MESH,
            )
        )
        third[-1].start()
    for copy in third:
        copy.wait_recv()
    shared = factor.shape[0]
    lane = lax.broadcasted_iota(jnp.int32, (shared, shared), 1)
    row = lax.broadcasted_iota(jnp.int32, (shared, shared), 0)
    value = jnp.concatenate([whole[:, :shared], whole[:, shared:]], 0)
    value = value * scale + jnp.where(lane == row, prior[...], 0.0)
    factor[...] = jnp.concatenate(eliminate([value], 0)[0], 0)
    for copy in first + second + third:
        copy.wait_send()
    rows.wait()


def factor_scenes(panel, offsets, damping, sens, parts, out, info, spread_sens):
    own, width, _ = info.shape
    spline = out.shape[1]
    half = width // 2
    beyond = width - spline
    for q in range(own):
        wide = jnp.concatenate([sens[q], jnp.zeros((spline, beyond), BF16)], 1)
        spread_sens[q] = jnp.concatenate([wide, jnp.zeros((beyond, width), BF16)], 0)
    row_index = lax.broadcasted_iota(jnp.int32, (width, width), 0)
    lane = lax.broadcasted_iota(jnp.int32, (width, width), 1)
    on_diagonal = (row_index == lane) & (row_index < spline)
    across = lane[:half, :half] - row_index[:half, :half]
    for q in range(own):
        packed = sum(
            part[q - offset]
            for offset, part in zip(offsets, parts)
            if offset <= q < offset + part.shape[0]
        )
        side, both = packed[:half], packed[half : 2 * half]
        upper = jnp.where(across > 0, both, 0.0)
        first = jnp.where(across >= 0, both, upper.T)
        lower = jnp.where(across < 0, both, 0.0)
        last = lower + jnp.where(across == 0, packed[2 * half : 2 * half + 1], lower.T)
        top = jnp.concatenate([first, side], 1)
        bottom = jnp.concatenate([side.T, last], 1)
        whole = jnp.concatenate([top, bottom], 0)
        s = spread_sens[q]
        mixed = whole + sum(
            jnp.dot(piece, s, preferred_element_type=F32) for piece in two_parts(whole)
        )
        result = mixed + sum(over_rows(s, piece) for piece in two_parts(mixed))
        info[q] = result + jnp.where(on_diagonal, damping[q], 0.0)
    for start in range(0, spline, panel):
        base = start // LANES * LANES
        panels = [info[q, start : start + panel, base:] for q in range(own)]
        rows = eliminate(panels, start - base)
        if base:
            out[:, start : start + panel, :base] = jnp.zeros((own, panel, base), F32)
        after = start + panel
        for q in range(own):
            block = jnp.concatenate(rows[q], 0)
            out[q, start : start + panel, base:] = block
            high, low = two_parts(block)
            left = jnp.concatenate([high, high, low], 0)
            right = jnp.concatenate([high, low, high], 0)
            for top in range(after // LANES * LANES, width, LANES):
                skip = max(after - top, 0)
                update = over_rows(left[:, top - base : top - base + LANES], right[:, top - base :])
                info[q, top + skip : top + LANES, top:] -= update[skip:]
    total = info[0, spline:, half:]
    for q in range(1, own):
        total = total + info[q, spline:, half:]
    total = total[:, spline - half :]
    middle = (width - spline) // 2
    return jnp.concatenate([total[:middle], total[middle:]], 1)


def finish(parts, sensitivity, damping, prior, width, axes):
    own = damping.shape[0]
    spline = sensitivity.shape[1]
    beyond = width - spline
    (_, n), (_, groups) = axes
    mine = lax.dynamic_slice_in_dim(sensitivity, lax.axis_index("tie") * own, own)
    offsets = [offset for offset, _ in parts]
    scale = 1.0 / (own * n * groups)
    block = (beyond // 2 // n, 2 * beyond)
    dma = pltpu.SemaphoreType.DMA
    return pl.pallas_call(
        functools.partial(finish_kernel, PANEL, offsets, axes, scale),
        in_specs=[pl.BlockSpec(memory_space=pltpu.SMEM)] + [VMEM] * (2 + len(parts)),
        out_specs=[pl.BlockSpec(memory_space=pl.ANY), VMEM],
        scratch_shapes=[
            pltpu.VMEM((own, width, width), F32),
            pltpu.VMEM((own, width, width), BF16),
            pltpu.VMEM((own, spline, width), F32),
            pltpu.VMEM((beyond // 2, 2 * beyond), F32),
            pltpu.VMEM((n,) + block, F32),
            pltpu.VMEM((groups,) + block, F32),
            pltpu.VMEM((beyond // 2, 2 * beyond), F32),
            dma,
            dma((n,)),
            dma((n,)),
            dma((groups,)),
            dma((groups,)),
            dma((n,)),
            dma((n,)),
        ],
        out_shape=[
            jax.ShapeDtypeStruct((own, spline, width), F32),
            jax.ShapeDtypeStruct((beyond, beyond), F32),
        ],
        compiler_params=pltpu.CompilerParams(
            collective_id=0, has_side_effects=True, vmem_limit_bytes=32 << 20
        ),
        name="finish",
    )(damping, mine, prior[None, :], *(part for _, part in parts))


def emit_kernel(rows, factor, rows_out, factor_out, sems):
    copies = [
        pltpu.make_async_copy(rows, rows_out, sems.at[0]),
        pltpu.make_async_copy(factor, factor_out, sems.at[1]),
    ]
    for copy in copies:
        copy.start()
    for copy in copies:
        copy.wait()


def emit(scene_rows, factor):
    anywhere = pl.BlockSpec(memory_space=pl.ANY)
    return pl.pallas_call(
        emit_kernel,
        in_specs=[anywhere] * 2,
        out_specs=[anywhere] * 2,
        scratch_shapes=[pltpu.SemaphoreType.DMA((2,))],
        out_shape=[jax.ShapeDtypeStruct(x.shape, x.dtype) for x in (scene_rows, factor)],
        compiler_params=pltpu.CompilerParams(vmem_limit_bytes=1 << 20),
        name="emit",
    )(scene_rows, factor)


def on_device(axes, tie_rows, point_counts, pattern, sensitivity, damping, prior):
    sizes = dict(axes)
    own = damping.shape[0]
    width = tie_rows.shape[2]
    parts = merged_sums(tie_rows, point_counts, pattern, own, sizes["tie"])
    return emit(*finish(parts, sensitivity, damping, prior, width, axes))


def solution(mesh):
    axes = (("tie", mesh.shape["tie"]), ("scene", mesh.shape["scene"]))
    placed = (
        P("tie", None, None),
        P("tie"),
        P("scene", "tie"),
        P("scene", None, None),
        P(("scene", "tie")),
        P(),
    )
    return jax.shard_map(
        functools.partial(on_device, axes),
        mesh=mesh,
        in_specs=placed,
        out_specs=(P(("scene", "tie"), None, None), P()),
        check_vma=False,
    )
```

```python
import functools

import jax
import jax.numpy as jnp
from jax import lax
from jax.experimental import pallas as pl
from jax.experimental.pallas import tpu as pltpu
from jax.sharding import PartitionSpec as P


MESH = pl.DeviceIdType.MESH
F32 = jnp.float32
BF16 = jnp.bfloat16
PANEL = 32
LANES = 128
SUB = 8
UNROLL = 8
DEPTH = 32
PIECES = 2
VMEM = pl.BlockSpec(memory_space=pltpu.VMEM)


def over_rows(a, b):
    return lax.dot_general(a, b, (((0,), (0,)), ((), ())), preferred_element_type=F32)


def gram_kernel(groups, own, pairs, counts, pattern, rows, *rest):
    outs = rest[: len(groups)]
    ring, acc, entries, arrived = rest[len(groups) :]
    depth, _, wide = ring.shape
    half = wide // 2
    total = pattern.shape[1]
    stride = 1 << (total - 1).bit_length()
    me = lax.axis_index("tie")

    def fetch(n):
        at = lax.rem(n, depth)
        block = entries[n] & (stride - 1)
        return pltpu.make_async_copy(rows.at[block], ring.at[at], arrived.at[at])

    def start_fetch(n, carry):
        fetch(n).start()
        return carry

    filled = jnp.int32(0)
    place = 0
    for hop, side, offset, size in groups:
        device = lax.rem(me // 2 + hop, pairs) * 2 + lax.rem(me + side, 2)

        def scan(q, n, device=device, offset=offset, place=place):
            scene = device * own + offset + q
            base = (place + q) * stride
            was = n
            for block in range(total):
                entries[n] = base + block
                n = n + pattern[scene, block]
            lax.fori_loop(jnp.minimum(was, depth), jnp.minimum(n, depth), start_fetch, 0)
            return n

        filled = lax.fori_loop(0, size, scan, filled)
        place += size
    acc[...] = jnp.zeros_like(acc)
    reach = lax.broadcasted_iota(jnp.int32, (2 * SUB, wide), 1)

    def step(it, carry):
        for u in range(UNROLL):
            n = it * UNROLL + u

            @pl.when(n < filled)
            def _(n=n):
                fetch(n).wait()

        for u in range(UNROLL):
            n = it * UNROLL + u
            at = jnp.minimum(n, filled - 1)
            entry = entries[at]
            keep = jnp.where(n < filled, 2 * counts[entry & (stride - 1)], 0)
            value = ring[lax.rem(at, depth)]
            mask = jnp.where(reach < keep, 1.0, 0.0).astype(BF16)
            kept = value.T * jnp.concatenate([mask] * (wide // (2 * SUB)), 0)
            top = jnp.dot(kept[:half], value, preferred_element_type=F32)
            bottom = jnp.dot(kept[half:], value[:, half:], preferred_element_type=F32)
            to = entry // stride
            acc[to, :half] += top[:, :half]
            acc[to, half : 2 * half] += top[:, half:]
            acc[to, 2 * half :] += bottom
        for u in range(UNROLL):
            n = it * UNROLL + u + depth

            @pl.when(n < filled)
            def _(n=n):
                fetch(n).start()

        return carry

    lax.fori_loop(0, (filled + UNROLL - 1) // UNROLL, step, 0)
    row = lax.broadcasted_iota(jnp.int32, (half, half), 0)
    lane = lax.broadcasted_iota(jnp.int32, (half, half), 1)
    place = 0
    for out, (_, _, _, size) in zip(outs, groups):
        diagonals = [None] * size
        for q in range(size):
            low = acc[place, 2 * half :]
            at = q * wide
            out[at : at + half] = acc[place, half : 2 * half]
            out[at + half : at + wide] = jnp.where(row <= lane, acc[place, :half], low)
            diagonals[q] = jnp.sum(jnp.where(row == lane, low, 0.0), 0, keepdims=True)
            place += 1
        diagonals += [jnp.zeros((1, half), F32)] * (out.shape[0] - size * wide - size)
        out[size * wide :] = jnp.concatenate(diagonals, 0)


def gram_sums(tie_rows, point_counts, pattern, groups, own, n):
    total, height, wide = tie_rows.shape
    half = wide // 2
    sizes = [group[3] for group in groups]
    most = sum(sizes)
    smem = pl.BlockSpec(memory_space=pltpu.SMEM)
    return pl.pallas_call(
        functools.partial(gram_kernel, groups, own, n // 2),
        in_specs=[smem, smem, pl.BlockSpec(memory_space=pl.ANY)],
        out_specs=[VMEM] * len(sizes),
        out_shape=[
            jax.ShapeDtypeStruct((size * wide + -(-size // SUB) * SUB, half), F32) for size in sizes
        ],
        scratch_shapes=[
            pltpu.VMEM((DEPTH, height, wide), BF16),
            pltpu.VMEM((most, 3 * half, half), F32),
            pltpu.SMEM((most * total + 1,), jnp.int32),
            pltpu.SemaphoreType.DMA((DEPTH,)),
        ],
        compiler_params=pltpu.CompilerParams(vmem_limit_bytes=16 << 20),
    )(point_counts, pattern, tie_rows)


def join_kernel(x, y, out):
    out[...] = x[...] + y[...]


def join(x, y):
    return pl.pallas_call(
        join_kernel,
        in_specs=[VMEM] * 2,
        out_specs=VMEM,
        out_shape=jax.ShapeDtypeStruct(x.shape, F32),
        compiler_params=pltpu.CompilerParams(vmem_limit_bytes=4 << 20),
        name="join",
    )(x, y)


def swap_cores(x, n):
    return lax.ppermute(x, "tie", [(t, t ^ 1) for t in range(n)])


def send_over(x, n, hop):
    pairs = n // 2
    return lax.ppermute(x, "tie", [(t, (t // 2 + hop) % pairs * 2 + t % 2) for t in range(n)])


def merged_sums(tie_rows, point_counts, pattern, own, n):
    size = own // PIECES
    parts = []
    tie_rows, point_counts, pattern = (
        pltpu.with_memory_space_constraint(x, pltpu.HBM) for x in (tie_rows, point_counts, pattern)
    )
    for hop in range(1, n // 2):
        for offset in range(0, own, size):
            groups = [(hop, side, offset, size) for side in (1, 0)]
            theirs, mine = gram_sums(tie_rows, point_counts, pattern, groups, own, n)
            both = join(mine, swap_cores(theirs, n))
            both, point_counts = lax.optimization_barrier((both, point_counts))
            parts.append((offset, send_over(both, n, hop)))
    groups = [(0, 1, 0, own), (0, 0, 0, own)]
    theirs, mine = gram_sums(tie_rows, point_counts, pattern, groups, own, n)
    return [(0, mine), (0, swap_cores(theirs, n))] + parts


def two_parts(x):
    high = x.astype(BF16)
    return high, (x - high.astype(F32)).astype(BF16)


def eliminate(panels, first):
    height, wide = panels[0].shape
    tile = (SUB, LANES)
    count = height // SUB
    rows = [[p[SUB * h : SUB * (h + 1)] for h in range(count)] for p in panels]
    row_index = lax.broadcasted_iota(jnp.int32, (SUB, wide), 0)
    lane = lax.broadcasted_iota(jnp.int32, (SUB, wide), 1)
    tile_row = lax.broadcasted_iota(jnp.int32, tile, 0)
    below = [tile_row > k for k in range(SUB)]

    def spread(x):
        return x if wide == LANES else (jnp.concatenate([x] * (wide // LANES), 1) if wide > LANES else x[:, :wide])

    for g in range(count):
        start = first + SUB * g
        cols = [
            [[jnp.broadcast_to(r[h][:, start + m : start + m + 1], tile) for h in range(g, count)] for m in range(SUB)]
            for r in rows
        ]
        for q, r in enumerate(rows):
            b = cols[q]
            pivots = b[0][0]
            for k in range(SUB):
                inverse = 1.0 / b[k][0][k : k + 1]
                pivots = jnp.where(tile_row == k, b[k][0], pivots)
                scaled = r[g][k : k + 1] * spread(inverse)
                factors = [b[m][0][k : k + 1] * inverse for m in range(k + 1, SUB)]
                for h in range(g, count):
                    column = b[k][h - g]
                    if h == g:
                        if k == SUB - 1:
                            continue
                        column = jnp.where(below[k], column, 0.0)
                    for m in range(k + 1, SUB):
                        b[m][h - g] = b[m][h - g] - column * factors[m - k - 1]
                    r[h] = r[h] - spread(column) * scaled
            r[g] = jnp.where(lane >= row_index + start, r[g] * spread(lax.rsqrt(pivots)), 0.0)
    return rows


def exchange(ref, slots, send, recv, name, n, width=None):
    me = lax.axis_index(name)
    copies = []
    for k in range(1, n):
        other = lax.rem(me + k, n)
        part = ref if width is None else ref.at[pl.ds(pl.multiple_of(other * width, width), width)]
        copies.append(
            pltpu.make_async_remote_copy(
                src_ref=part,
                dst_ref=slots.at[k],
                send_sem=send.at[k],
                recv_sem=recv.at[k],
                device_id={name: other},
                device_id_type=MESH,
            )
        )
        copies[-1].start()
    return copies


def added(slots, name, n):
    me = lax.axis_index(name)
    acc = slots[me]
    for i in range(1, n):
        acc = acc + slots[lax.rem(me - i + n, n)]
    return acc


def finish_kernel(panel, offsets, axes, scale, damping, sens, prior, *rest):
    parts = rest[: len(offsets)]
    scene_rows, factor, info, spread_sens, out = rest[len(offsets) : len(offsets) + 5]
    mine, near, wide_slots, whole, written, s1, r1, s2, r2, s3, r3 = rest[len(offsets) + 5 :]
    barrier = pltpu.get_barrier_semaphore()
    for name, n in axes:
        me = lax.axis_index(name)
        for k in range(1, n):
            pl.semaphore_signal(
                barrier, inc=1, device_id={name: lax.rem(me + k, n)}, device_id_type=MESH
            )
    mine[...] = factor_scenes(panel, offsets, damping, sens, parts, out, info, spread_sens)
    rows = pltpu.make_async_copy(out, scene_rows, written)
    rows.start()
    pl.semaphore_wait(barrier, sum(n - 1 for _, n in axes))
    (tie, n), (scene, groups) = axes
    chunk = mine.shape[0] // n
    me = lax.axis_index(tie)
    own = pl.ds(pl.multiple_of(me * chunk, chunk), chunk)
    near[0] = mine[own]
    first = exchange(mine, near, s1, r1, tie, n, chunk)
    for copy in first:
        copy.wait_recv()
    wide_slots[0] = added(near, tie, n)
    second = exchange(wide_slots.at[0], wide_slots, s2, r2, scene, groups)
    for copy in second:
        copy.wait_recv()
    whole[own] = added(wide_slots, scene, groups)
    third = []
    for k in range(1, n):
        third.append(
            pltpu.make_async_remote_copy(
                src_ref=whole.at[own],
                dst_ref=whole.at[own],
                send_sem=s3.at[k],
                recv_sem=r3.at[k],
                device_id={tie: lax.rem(me + k, n)},
                device_id_type=MESH,
            )
        )
        third[-1].start()
    for copy in third:
        copy.wait_recv()
    shared = factor.shape[0]
    lane = lax.broadcasted_iota(jnp.int32, (shared, shared), 1)
    row = lax.broadcasted_iota(jnp.int32, (shared, shared), 0)
    value = jnp.concatenate([whole[:, :shared], whole[:, shared:]], 0)
    value = value * scale + jnp.where(lane == row, prior[...], 0.0)
    factor[...] = jnp.concatenate(eliminate([value], 0)[0], 0)
    for copy in first + second + third:
        copy.wait_send()
    rows.wait()


def factor_scenes(panel, offsets, damping, sens, parts, out, info, spread_sens):
    own, width, _ = info.shape
    spline = out.shape[1]
    half = width // 2
    beyond = width - spline
    for q in range(own):
        wide = jnp.concatenate([sens[q], jnp.zeros((spline, beyond), BF16)], 1)
        spread_sens[q] = jnp.concatenate([wide, jnp.zeros((beyond, width), BF16)], 0)
    row_index = lax.broadcasted_iota(jnp.int32, (width, width), 0)
    lane = lax.broadcasted_iota(jnp.int32, (width, width), 1)
    on_diagonal = (row_index == lane) & (row_index < spline)
    across = lane[:half, :half] - row_index[:half, :half]
    for q in range(own):
        held = [
            (part, q - offset, part.shape[0] // width)
            for offset, part in zip(offsets, parts)
            if offset <= q < offset + part.shape[0] // width
        ]
        packed = sum(part[at * width : (at + 1) * width] for part, at, _ in held)
        diagonal = sum(part[size * width + at : size * width + at + 1] for part, at, size in held)
        side, both = packed[:half], packed[half:]
        upper = jnp.where(across > 0, both, 0.0)
        first = jnp.where(across >= 0, both, upper.T)
        lower = jnp.where(across < 0, both, 0.0)
        last = lower + jnp.where(across == 0, diagonal, lower.T)
        top = jnp.concatenate([first, side], 1)
        bottom = jnp.concatenate([side.T, last], 1)
        whole = jnp.concatenate([top, bottom], 0)
        s = spread_sens[q]
        mixed = whole + sum(
            jnp.dot(piece, s, preferred_element_type=F32) for piece in two_parts(whole)
        )
        result = mixed + sum(over_rows(s, piece) for piece in two_parts(mixed))
        info[q] = result + jnp.where(on_diagonal, damping[q], 0.0)
    for start in range(0, spline, panel):
        base = start // LANES * LANES
        panels = [info[q, start : start + panel, base:] for q in range(own)]
        rows = eliminate(panels, start - base)
        if base:
            out[:, start : start + panel, :base] = jnp.zeros((own, panel, base), F32)
        after = start + panel
        for q in range(own):
            block = jnp.concatenate(rows[q], 0)
            out[q, start : start + panel, base:] = block
            high, low = two_parts(block)
            left = jnp.concatenate([high, high, low], 0)
            right = jnp.concatenate([high, low, high], 0)
            for top in range(after // LANES * LANES, width, LANES):
                skip = max(after - top, 0)
                update = over_rows(left[:, top - base : top - base + LANES], right[:, top - base :])
                info[q, top + skip : top + LANES, top:] -= update[skip:]
    total = info[0, spline:, half:]
    for q in range(1, own):
        total = total + info[q, spline:, half:]
    total = total[:, spline - half :]
    middle = (width - spline) // 2
    return jnp.concatenate([total[:middle], total[middle:]], 1)


def finish(parts, sensitivity, damping, prior, width, axes):
    own = damping.shape[0]
    spline = sensitivity.shape[1]
    beyond = width - spline
    (_, n), (_, groups) = axes
    mine = lax.dynamic_slice_in_dim(sensitivity, lax.axis_index("tie") * own, own)
    offsets = [offset for offset, _ in parts]
    scale = 1.0 / (own * n * groups)
    block = (beyond // 2 // n, 2 * beyond)
    dma = pltpu.SemaphoreType.DMA
    return pl.pallas_call(
        functools.partial(finish_kernel, PANEL, offsets, axes, scale),
        in_specs=[pl.BlockSpec(memory_space=pltpu.SMEM)] + [VMEM] * (2 + len(parts)),
        out_specs=[pl.BlockSpec(memory_space=pl.ANY), VMEM],
        scratch_shapes=[
            pltpu.VMEM((own, width, width), F32),
            pltpu.VMEM((own, width, width), BF16),
            pltpu.VMEM((own, spline, width), F32),
            pltpu.VMEM((beyond // 2, 2 * beyond), F32),
            pltpu.VMEM((n,) + block, F32),
            pltpu.VMEM((groups,) + block, F32),
            pltpu.VMEM((beyond // 2, 2 * beyond), F32),
            dma,
            dma((n,)),
            dma((n,)),
            dma((groups,)),
            dma((groups,)),
            dma((n,)),
            dma((n,)),
        ],
        out_shape=[
            jax.ShapeDtypeStruct((own, spline, width), F32),
            jax.ShapeDtypeStruct((beyond, beyond), F32),
        ],
        compiler_params=pltpu.CompilerParams(
            collective_id=0, has_side_effects=True, vmem_limit_bytes=32 << 20
        ),
        name="finish",
    )(damping, mine, prior[None, :], *(part for _, part in parts))


def emit_kernel(rows, factor, rows_out, factor_out, sems):
    copies = [
        pltpu.make_async_copy(rows, rows_out, sems.at[0]),
        pltpu.make_async_copy(factor, factor_out, sems.at[1]),
    ]
    for copy in copies:
        copy.start()
    for copy in copies:
        copy.wait()


def emit(scene_rows, factor):
    anywhere = pl.BlockSpec(memory_space=pl.ANY)
    return pl.pallas_call(
        emit_kernel,
        in_specs=[anywhere] * 2,
        out_specs=[anywhere] * 2,
        scratch_shapes=[pltpu.SemaphoreType.DMA((2,))],
        out_shape=[jax.ShapeDtypeStruct(x.shape, x.dtype) for x in (scene_rows, factor)],
        compiler_params=pltpu.CompilerParams(vmem_limit_bytes=1 << 20),
        name="emit",
    )(scene_rows, factor)


def on_device(axes, tie_rows, point_counts, pattern, sensitivity, damping, prior):
    sizes = dict(axes)
    own = damping.shape[0]
    width = tie_rows.shape[2]
    parts = merged_sums(tie_rows, point_counts, pattern, own, sizes["tie"])
    return emit(*finish(parts, sensitivity, damping, prior, width, axes))


def solution(mesh):
    axes = (("tie", mesh.shape["tie"]), ("scene", mesh.shape["scene"]))
    placed = (
        P("tie", None, None),
        P("tie"),
        P("scene", "tie"),
        P("scene", None, None),
        P(("scene", "tie")),
        P(),
    )
    return jax.shard_map(
        functools.partial(on_device, axes),
        mesh=mesh,
        in_specs=placed,
        out_specs=(P(("scene", "tie"), None, None), P()),
        check_vma=False,
    )
```

```python
import functools

import jax
import jax.numpy as jnp
from jax import lax
from jax.experimental import pallas as pl
from jax.experimental.pallas import tpu as pltpu
from jax.sharding import PartitionSpec as P


MESH = pl.DeviceIdType.MESH
F32 = jnp.float32
BF16 = jnp.bfloat16
PANEL = 32
LANES = 128
SUB = 8
UNROLL = 8
DEPTH = 32
PIECES = 2
VMEM = pl.BlockSpec(memory_space=pltpu.VMEM)


def over_rows(a, b):
    return lax.dot_general(a, b, (((0,), (0,)), ((), ())), preferred_element_type=F32)


def gram_kernel(groups, own, pairs, counts, pattern, rows, *rest):
    outs = rest[: len(groups)]
    ring, acc, entries, arrived = rest[len(groups) :]
    depth, _, wide = ring.shape
    half = wide // 2
    total = pattern.shape[1]
    stride = 1 << (total - 1).bit_length()
    me = lax.axis_index("tie")

    def fetch(n):
        at = lax.rem(n, depth)
        block = entries[n] & (stride - 1)
        return pltpu.make_async_copy(rows.at[block], ring.at[at], arrived.at[at])

    def start_fetch(n, carry):
        fetch(n).start()
        return carry

    filled = jnp.int32(0)
    place = 0
    for hop, side, offset, size in groups:
        device = lax.rem(me // 2 + hop, pairs) * 2 + lax.rem(me + side, 2)

        def scan(q, n, device=device, offset=offset, place=place):
            scene = device * own + offset + q
            base = (place + q) * stride
            was = n
            for block in range(total):
                entries[n] = base + block
                n = n + pattern[scene, block]
            lax.fori_loop(jnp.minimum(was, depth), jnp.minimum(n, depth), start_fetch, 0)
            return n

        filled = lax.fori_loop(0, size, scan, filled)
        place += size
    acc[...] = jnp.zeros_like(acc)
    reach = lax.broadcasted_iota(jnp.int32, (2 * SUB, wide), 1)

    def step(it, carry):
        for u in range(UNROLL):
            n = it * UNROLL + u

            @pl.when(n < filled)
            def _(n=n):
                fetch(n).wait()

        for u in range(UNROLL):
            n = it * UNROLL + u
            at = jnp.minimum(n, filled - 1)
            entry = entries[at]
            keep = jnp.where(n < filled, 2 * counts[entry & (stride - 1)], 0)
            value = ring[lax.rem(at, depth)]
            mask = jnp.where(reach < keep, 1.0, 0.0).astype(BF16)
            kept = value.T * jnp.concatenate([mask] * (wide // (2 * SUB)), 0)
            top = jnp.dot(kept[:half], value, preferred_element_type=F32)
            bottom = jnp.dot(kept[half:], value[:, half:], preferred_element_type=F32)
            to = entry // stride
            acc[to, :half] += top[:, :half]
            acc[to, half : 2 * half] += top[:, half:]
            acc[to, 2 * half :] += bottom
        for u in range(UNROLL):
            n = it * UNROLL + u + depth

            @pl.when(n < filled)
            def _(n=n):
                fetch(n).start()

        return carry

    lax.fori_loop(0, (filled + UNROLL - 1) // UNROLL, step, 0)
    row = lax.broadcasted_iota(jnp.int32, (half, half), 0)
    lane = lax.broadcasted_iota(jnp.int32, (half, half), 1)
    place = 0
    for out, (_, _, _, size) in zip(outs, groups):
        diagonals = [None] * size
        for q in range(size):
            low = acc[place, 2 * half :]
            at = q * wide
            out[at : at + half] = acc[place, half : 2 * half]
            out[at + half : at + wide] = jnp.where(row <= lane, acc[place, :half], low)
            diagonals[q] = jnp.sum(jnp.where(row == lane, low, 0.0), 0, keepdims=True)
            place += 1
        diagonals += [jnp.zeros((1, half), F32)] * (out.shape[0] - size * wide - size)
        out[size * wide :] = jnp.concatenate(diagonals, 0)


def gram_sums(tie_rows, point_counts, pattern, groups, own, n):
    total, height, wide = tie_rows.shape
    half = wide // 2
    sizes = [group[3] for group in groups]
    most = sum(sizes)
    smem = pl.BlockSpec(memory_space=pltpu.SMEM)
    return pl.pallas_call(
        functools.partial(gram_kernel, groups, own, n // 2),
        in_specs=[smem, smem, pl.BlockSpec(memory_space=pl.ANY)],
        out_specs=[VMEM] * len(sizes),
        out_shape=[
            jax.ShapeDtypeStruct((size * wide + -(-size // SUB) * SUB, half), F32) for size in sizes
        ],
        scratch_shapes=[
            pltpu.VMEM((DEPTH, height, wide), BF16),
            pltpu.VMEM((most, 3 * half, half), F32),
            pltpu.SMEM((most * total + 1,), jnp.int32),
            pltpu.SemaphoreType.DMA((DEPTH,)),
        ],
        compiler_params=pltpu.CompilerParams(vmem_limit_bytes=16 << 20),
    )(point_counts, pattern, tie_rows)


def join_kernel(x, y, out):
    out[...] = x[...] + y[...]


def join(x, y):
    return pl.pallas_call(
        join_kernel,
        in_specs=[VMEM] * 2,
        out_specs=VMEM,
        out_shape=jax.ShapeDtypeStruct(x.shape, F32),
        compiler_params=pltpu.CompilerParams(vmem_limit_bytes=4 << 20),
        name="join",
    )(x, y)


def swap_cores(x, n):
    return lax.ppermute(x, "tie", [(t, t ^ 1) for t in range(n)])


def send_over(x, n, hop):
    pairs = n // 2
    return lax.ppermute(x, "tie", [(t, (t // 2 + hop) % pairs * 2 + t % 2) for t in range(n)])


def merged_sums(tie_rows, point_counts, pattern, own, n):
    size = own // PIECES
    parts = []
    tie_rows, point_counts, pattern = (
        pltpu.with_memory_space_constraint(x, pltpu.HBM) for x in (tie_rows, point_counts, pattern)
    )
    sends = [(hop, offset) for hop in range(1, n // 2) for offset in range(0, own, size)]
    near = [(0, 1, 0, own)]
    for k, (hop, offset) in enumerate(sends):
        groups = [(hop, side, offset, size) for side in (1, 0)]
        if k == len(sends) - 1:
            groups += near
        sums = gram_sums(tie_rows, point_counts, pattern, groups, own, n)
        both = join(sums[1], swap_cores(sums[0], n))
        both, point_counts = lax.optimization_barrier((both, point_counts))
        parts.append((offset, send_over(both, n, hop)))
    if sends:
        theirs = sums[2]
        (mine,) = gram_sums(tie_rows, point_counts, pattern, [(0, 0, 0, own)], own, n)
    else:
        groups = near + [(0, 0, 0, own)]
        theirs, mine = gram_sums(tie_rows, point_counts, pattern, groups, own, n)
    return [(0, mine), (0, swap_cores(theirs, n))] + parts


def two_parts(x):
    high = x.astype(BF16)
    return high, (x - high.astype(F32)).astype(BF16)


def eliminate(panels, first):
    height, wide = panels[0].shape
    tile = (SUB, LANES)
    count = height // SUB
    rows = [[p[SUB * h : SUB * (h + 1)] for h in range(count)] for p in panels]
    row_index = lax.broadcasted_iota(jnp.int32, (SUB, wide), 0)
    lane = lax.broadcasted_iota(jnp.int32, (SUB, wide), 1)
    tile_row = lax.broadcasted_iota(jnp.int32, tile, 0)
    below = [tile_row > k for k in range(SUB)]

    def spread(x):
        return x if wide == LANES else (jnp.concatenate([x] * (wide // LANES), 1) if wide > LANES else x[:, :wide])

    for g in range(count):
        start = first + SUB * g
        cols = [
            [[jnp.broadcast_to(r[h][:, start + m : start + m + 1], tile) for h in range(g, count)] for m in range(SUB)]
            for r in rows
        ]
        for q, r in enumerate(rows):
            b = cols[q]
            pivots = b[0][0]
            for k in range(SUB):
                inverse = 1.0 / b[k][0][k : k + 1]
                pivots = jnp.where(tile_row == k, b[k][0], pivots)
                scaled = r[g][k : k + 1] * spread(inverse)
                factors = [b[m][0][k : k + 1] * inverse for m in range(k + 1, SUB)]
                for h in range(g, count):
                    column = b[k][h - g]
                    if h == g:
                        if k == SUB - 1:
                            continue
                        column = jnp.where(below[k], column, 0.0)
                    for m in range(k + 1, SUB):
                        b[m][h - g] = b[m][h - g] - column * factors[m - k - 1]
                    r[h] = r[h] - spread(column) * scaled
            r[g] = jnp.where(lane >= row_index + start, r[g] * spread(lax.rsqrt(pivots)), 0.0)
    return rows


def exchange(ref, slots, send, recv, name, n, width=None):
    me = lax.axis_index(name)
    copies = []
    for k in range(1, n):
        other = lax.rem(me + k, n)
        part = ref if width is None else ref.at[pl.ds(pl.multiple_of(other * width, width), width)]
        copies.append(
            pltpu.make_async_remote_copy(
                src_ref=part,
                dst_ref=slots.at[k],
                send_sem=send.at[k],
                recv_sem=recv.at[k],
                device_id={name: other},
                device_id_type=MESH,
            )
        )
        copies[-1].start()
    return copies


def added(slots, name, n):
    me = lax.axis_index(name)
    acc = slots[me]
    for i in range(1, n):
        acc = acc + slots[lax.rem(me - i + n, n)]
    return acc


def finish_kernel(panel, offsets, axes, scale, damping, sens, prior, *rest):
    parts = rest[: len(offsets)]
    scene_rows, factor, info, spread_sens, out = rest[len(offsets) : len(offsets) + 5]
    mine, near, wide_slots, whole, written, s1, r1, s2, r2, s3, r3 = rest[len(offsets) + 5 :]
    barrier = pltpu.get_barrier_semaphore()
    for name, n in axes:
        me = lax.axis_index(name)
        for k in range(1, n):
            pl.semaphore_signal(
                barrier, inc=1, device_id={name: lax.rem(me + k, n)}, device_id_type=MESH
            )
    mine[...] = factor_scenes(panel, offsets, damping, sens, parts, out, info, spread_sens)
    rows = pltpu.make_async_copy(out, scene_rows, written)
    rows.start()
    pl.semaphore_wait(barrier, sum(n - 1 for _, n in axes))
    (tie, n), (scene, groups) = axes
    chunk = mine.shape[0] // n
    me = lax.axis_index(tie)
    own = pl.ds(pl.multiple_of(me * chunk, chunk), chunk)
    near[0] = mine[own]
    first = exchange(mine, near, s1, r1, tie, n, chunk)
    for copy in first:
        copy.wait_recv()
    wide_slots[0] = added(near, tie, n)
    second = exchange(wide_slots.at[0], wide_slots, s2, r2, scene, groups)
    for copy in second:
        copy.wait_recv()
    whole[own] = added(wide_slots, scene, groups)
    third = []
    for k in range(1, n):
        third.append(
            pltpu.make_async_remote_copy(
                src_ref=whole.at[own],
                dst_ref=whole.at[own],
                send_sem=s3.at[k],
                recv_sem=r3.at[k],
                device_id={tie: lax.rem(me + k, n)},
                device_id_type=MESH,
            )
        )
        third[-1].start()
    for copy in third:
        copy.wait_recv()
    shared = factor.shape[0]
    lane = lax.broadcasted_iota(jnp.int32, (shared, shared), 1)
    row = lax.broadcasted_iota(jnp.int32, (shared, shared), 0)
    value = jnp.concatenate([whole[:, :shared], whole[:, shared:]], 0)
    value = value * scale + jnp.where(lane == row, prior[...], 0.0)
    factor[...] = jnp.concatenate(eliminate([value], 0)[0], 0)
    for copy in first + second + third:
        copy.wait_send()
    rows.wait()


def factor_scenes(panel, offsets, damping, sens, parts, out, info, spread_sens):
    own, width, _ = info.shape
    spline = out.shape[1]
    half = width // 2
    beyond = width - spline
    for q in range(own):
        wide = jnp.concatenate([sens[q], jnp.zeros((spline, beyond), BF16)], 1)
        spread_sens[q] = jnp.concatenate([wide, jnp.zeros((beyond, width), BF16)], 0)
    row_index = lax.broadcasted_iota(jnp.int32, (width, width), 0)
    lane = lax.broadcasted_iota(jnp.int32, (width, width), 1)
    on_diagonal = (row_index == lane) & (row_index < spline)
    across = lane[:half, :half] - row_index[:half, :half]
    for q in range(own):
        held = [
            (part, q - offset, part.shape[0] // width)
            for offset, part in zip(offsets, parts)
            if offset <= q < offset + part.shape[0] // width
        ]
        packed = sum(part[at * width : (at + 1) * width] for part, at, _ in held)
        diagonal = sum(part[size * width + at : size * width + at + 1] for part, at, size in held)
        side, both = packed[:half], packed[half:]
        upper = jnp.where(across > 0, both, 0.0)
        first = jnp.where(across >= 0, both, upper.T)
        lower = jnp.where(across < 0, both, 0.0)
        last = lower + jnp.where(across == 0, diagonal, lower.T)
        top = jnp.concatenate([first, side], 1)
        bottom = jnp.concatenate([side.T, last], 1)
        whole = jnp.concatenate([top, bottom], 0)
        s = spread_sens[q]
        mixed = whole + sum(
            jnp.dot(piece, s, preferred_element_type=F32) for piece in two_parts(whole)
        )
        result = mixed + sum(over_rows(s, piece) for piece in two_parts(mixed))
        info[q] = result + jnp.where(on_diagonal, damping[q], 0.0)
    for start in range(0, spline, panel):
        base = start // LANES * LANES
        panels = [info[q, start : start + panel, base:] for q in range(own)]
        rows = eliminate(panels, start - base)
        if base:
            out[:, start : start + panel, :base] = jnp.zeros((own, panel, base), F32)
        after = start + panel
        for q in range(own):
            block = jnp.concatenate(rows[q], 0)
            out[q, start : start + panel, base:] = block
            high, low = two_parts(block)
            left = jnp.concatenate([high, high, low], 0)
            right = jnp.concatenate([high, low, high], 0)
            for top in range(after // LANES * LANES, width, LANES):
                skip = max(after - top, 0)
                update = over_rows(left[:, top - base : top - base + LANES], right[:, top - base :])
                info[q, top + skip : top + LANES, top:] -= update[skip:]
    total = info[0, spline:, half:]
    for q in range(1, own):
        total = total + info[q, spline:, half:]
    total = total[:, spline - half :]
    middle = (width - spline) // 2
    return jnp.concatenate([total[:middle], total[middle:]], 1)


def finish(parts, sensitivity, damping, prior, width, axes):
    own = damping.shape[0]
    spline = sensitivity.shape[1]
    beyond = width - spline
    (_, n), (_, groups) = axes
    mine = lax.dynamic_slice_in_dim(sensitivity, lax.axis_index("tie") * own, own)
    offsets = [offset for offset, _ in parts]
    scale = 1.0 / (own * n * groups)
    block = (beyond // 2 // n, 2 * beyond)
    dma = pltpu.SemaphoreType.DMA
    return pl.pallas_call(
        functools.partial(finish_kernel, PANEL, offsets, axes, scale),
        in_specs=[pl.BlockSpec(memory_space=pltpu.SMEM)] + [VMEM] * (2 + len(parts)),
        out_specs=[pl.BlockSpec(memory_space=pl.ANY), VMEM],
        scratch_shapes=[
            pltpu.VMEM((own, width, width), F32),
            pltpu.VMEM((own, width, width), BF16),
            pltpu.VMEM((own, spline, width), F32),
            pltpu.VMEM((beyond // 2, 2 * beyond), F32),
            pltpu.VMEM((n,) + block, F32),
            pltpu.VMEM((groups,) + block, F32),
            pltpu.VMEM((beyond // 2, 2 * beyond), F32),
            dma,
            dma((n,)),
            dma((n,)),
            dma((groups,)),
            dma((groups,)),
            dma((n,)),
            dma((n,)),
        ],
        out_shape=[
            jax.ShapeDtypeStruct((own, spline, width), F32),
            jax.ShapeDtypeStruct((beyond, beyond), F32),
        ],
        compiler_params=pltpu.CompilerParams(
            collective_id=0, has_side_effects=True, vmem_limit_bytes=12 << 20
        ),
        name="finish",
    )(damping, mine, prior[None, :], *(part for _, part in parts))


def emit_kernel(rows, factor, rows_out, factor_out, sems):
    copies = [
        pltpu.make_async_copy(rows, rows_out, sems.at[0]),
        pltpu.make_async_copy(factor, factor_out, sems.at[1]),
    ]
    for copy in copies:
        copy.start()
    for copy in copies:
        copy.wait()


def emit(scene_rows, factor):
    anywhere = pl.BlockSpec(memory_space=pl.ANY)
    return pl.pallas_call(
        emit_kernel,
        in_specs=[anywhere] * 2,
        out_specs=[anywhere] * 2,
        scratch_shapes=[pltpu.SemaphoreType.DMA((2,))],
        out_shape=[jax.ShapeDtypeStruct(x.shape, x.dtype) for x in (scene_rows, factor)],
        compiler_params=pltpu.CompilerParams(vmem_limit_bytes=1 << 20),
        name="emit",
    )(scene_rows, factor)


def on_device(axes, tie_rows, point_counts, pattern, sensitivity, damping, prior):
    sizes = dict(axes)
    own = damping.shape[0]
    width = tie_rows.shape[2]
    parts = merged_sums(tie_rows, point_counts, pattern, own, sizes["tie"])
    return emit(*finish(parts, sensitivity, damping, prior, width, axes))


def solution(mesh):
    axes = (("tie", mesh.shape["tie"]), ("scene", mesh.shape["scene"]))
    placed = (
        P("tie", None, None),
        P("tie"),
        P("scene", "tie"),
        P("scene", None, None),
        P(("scene", "tie")),
        P(),
    )
    return jax.shard_map(
        functools.partial(on_device, axes),
        mesh=mesh,
        in_specs=placed,
        out_specs=(P(("scene", "tie"), None, None), P()),
        check_vma=False,
    )
```

```python
import functools

import jax
import jax.numpy as jnp
from jax import lax
from jax.experimental import pallas as pl
from jax.experimental.pallas import tpu as pltpu
from jax.sharding import PartitionSpec as P


MESH = pl.DeviceIdType.MESH
F32 = jnp.float32
BF16 = jnp.bfloat16
PANEL = 32
LANES = 128
SUB = 8
UNROLL = 8
DEPTH = 32
PIECES = 2
VMEM = pl.BlockSpec(memory_space=pltpu.VMEM)


def over_rows(a, b):
    return lax.dot_general(a, b, (((0,), (0,)), ((), ())), preferred_element_type=F32)


def gram_kernel(groups, own, pairs, counts, pattern, rows, *rest):
    outs = rest[: len(groups)]
    ring, acc, entries, arrived = rest[len(groups) :]
    depth, _, wide = ring.shape
    half = wide // 2
    total = pattern.shape[1]
    stride = 1 << (total - 1).bit_length()
    me = lax.axis_index("tie")

    def fetch(n):
        at = lax.rem(n, depth)
        block = entries[n] & (stride - 1)
        return pltpu.make_async_copy(rows.at[block], ring.at[at], arrived.at[at])

    def start_fetch(n, carry):
        fetch(n).start()
        return carry

    filled = jnp.int32(0)
    place = 0
    for hop, side, offset, size in groups:
        device = lax.rem(me // 2 + hop, pairs) * 2 + lax.rem(me + side, 2)

        def scan(q, n, device=device, offset=offset, place=place):
            scene = device * own + offset + q
            base = (place + q) * stride
            was = n
            for block in range(total):
                entries[n] = base + block
                n = n + pattern[scene, block]
            lax.fori_loop(jnp.minimum(was, depth), jnp.minimum(n, depth), start_fetch, 0)
            return n

        filled = lax.fori_loop(0, size, scan, filled)
        place += size
    acc[...] = jnp.zeros_like(acc)
    reach = lax.broadcasted_iota(jnp.int32, (2 * SUB, wide), 1)

    def step(it, carry):
        for u in range(UNROLL):
            n = it * UNROLL + u

            @pl.when(n < filled)
            def _(n=n):
                fetch(n).wait()

        for u in range(UNROLL):
            n = it * UNROLL + u
            at = jnp.minimum(n, filled - 1)
            entry = entries[at]
            keep = jnp.where(n < filled, 2 * counts[entry & (stride - 1)], 0)
            value = ring[lax.rem(at, depth)]
            mask = jnp.where(reach < keep, 1.0, 0.0).astype(BF16)
            kept = value.T * jnp.concatenate([mask] * (wide // (2 * SUB)), 0)
            top = jnp.dot(kept[:half], value, preferred_element_type=F32)
            bottom = jnp.dot(kept[half:], value[:, half:], preferred_element_type=F32)
            to = entry // stride
            acc[to, :half] += top[:, :half]
            acc[to, half : 2 * half] += top[:, half:]
            acc[to, 2 * half :] += bottom
        for u in range(UNROLL):
            n = it * UNROLL + u + depth

            @pl.when(n < filled)
            def _(n=n):
                fetch(n).start()

        return carry

    lax.fori_loop(0, (filled + UNROLL - 1) // UNROLL, step, 0)
    row = lax.broadcasted_iota(jnp.int32, (half, half), 0)
    lane = lax.broadcasted_iota(jnp.int32, (half, half), 1)
    place = 0
    for out, (_, _, _, size) in zip(outs, groups):
        diagonals = [None] * size
        for q in range(size):
            low = acc[place, 2 * half :]
            at = q * wide
            out[at : at + half] = acc[place, half : 2 * half]
            out[at + half : at + wide] = jnp.where(row <= lane, acc[place, :half], low)
            diagonals[q] = jnp.sum(jnp.where(row == lane, low, 0.0), 0, keepdims=True)
            place += 1
        diagonals += [jnp.zeros((1, half), F32)] * (out.shape[0] - size * wide - size)
        out[size * wide :] = jnp.concatenate(diagonals, 0)


def gram_sums(tie_rows, point_counts, pattern, groups, own, n):
    total, height, wide = tie_rows.shape
    half = wide // 2
    sizes = [group[3] for group in groups]
    most = sum(sizes)
    smem = pl.BlockSpec(memory_space=pltpu.SMEM)
    return pl.pallas_call(
        functools.partial(gram_kernel, groups, own, n // 2),
        in_specs=[smem, smem, pl.BlockSpec(memory_space=pl.ANY)],
        out_specs=[VMEM] * len(sizes),
        out_shape=[
            jax.ShapeDtypeStruct((size * wide + -(-size // SUB) * SUB, half), F32) for size in sizes
        ],
        scratch_shapes=[
            pltpu.VMEM((DEPTH, height, wide), BF16),
            pltpu.VMEM((most, 3 * half, half), F32),
            pltpu.SMEM((most * total + 1,), jnp.int32),
            pltpu.SemaphoreType.DMA((DEPTH,)),
        ],
        compiler_params=pltpu.CompilerParams(vmem_limit_bytes=16 << 20),
    )(point_counts, pattern, tie_rows)


def join_kernel(x, y, out):
    out[...] = x[...] + y[...]


def join(x, y):
    return pl.pallas_call(
        join_kernel,
        in_specs=[VMEM] * 2,
        out_specs=VMEM,
        out_shape=jax.ShapeDtypeStruct(x.shape, F32),
        compiler_params=pltpu.CompilerParams(vmem_limit_bytes=4 << 20),
        name="join",
    )(x, y)


def swap_cores(x, n):
    return lax.ppermute(x, "tie", [(t, t ^ 1) for t in range(n)])


def send_over(x, n, hop):
    pairs = n // 2
    return lax.ppermute(x, "tie", [(t, (t // 2 + hop) % pairs * 2 + t % 2) for t in range(n)])


def merged_sums(tie_rows, point_counts, pattern, own, n):
    size = own // PIECES
    parts = []
    tie_rows, point_counts, pattern = (
        pltpu.with_memory_space_constraint(x, pltpu.HBM) for x in (tie_rows, point_counts, pattern)
    )
    offsets = range(0, own, size)
    for hop in range(1, n // 2):
        groups = [(hop, side, offset, size) for side in (1, 0) for offset in offsets]
        sums = gram_sums(tie_rows, point_counts, pattern, groups, own, n)
        swapped = [swap_cores(theirs, n) for theirs in sums[: len(offsets)]]
        for offset, mine, theirs in zip(offsets, sums[len(offsets) :], swapped):
            both = join(mine, theirs)
            both, point_counts = lax.optimization_barrier((both, point_counts))
            parts.append((offset, send_over(both, n, hop)))
    groups = [(0, 1, offset, size) for offset in offsets] + [(0, 0, 0, own)]
    sums = gram_sums(tie_rows, point_counts, pattern, groups, own, n)
    swapped = [(o, swap_cores(theirs, n)) for o, theirs in zip(offsets, sums)]
    return [(0, sums[-1])] + swapped + parts


def two_parts(x):
    high = x.astype(BF16)
    return high, (x - high.astype(F32)).astype(BF16)


def eliminate(panels, first):
    height, wide = panels[0].shape
    tile = (SUB, LANES)
    count = height // SUB
    rows = [[p[SUB * h : SUB * (h + 1)] for h in range(count)] for p in panels]
    row_index = lax.broadcasted_iota(jnp.int32, (SUB, wide), 0)
    lane = lax.broadcasted_iota(jnp.int32, (SUB, wide), 1)
    tile_row = lax.broadcasted_iota(jnp.int32, tile, 0)
    below = [tile_row > k for k in range(SUB)]

    def spread(x):
        return x if wide == LANES else (jnp.concatenate([x] * (wide // LANES), 1) if wide > LANES else x[:, :wide])

    for g in range(count):
        start = first + SUB * g
        cols = [
            [[jnp.broadcast_to(r[h][:, start + m : start + m + 1], tile) for h in range(g, count)] for m in range(SUB)]
            for r in rows
        ]
        for q, r in enumerate(rows):
            b = cols[q]
            pivots = b[0][0]
            for k in range(SUB):
                inverse = 1.0 / b[k][0][k : k + 1]
                pivots = jnp.where(tile_row == k, b[k][0], pivots)
                scaled = r[g][k : k + 1] * spread(inverse)
                factors = [b[m][0][k : k + 1] * inverse for m in range(k + 1, SUB)]
                for h in range(g, count):
                    column = b[k][h - g]
                    if h == g:
                        if k == SUB - 1:
                            continue
                        column = jnp.where(below[k], column, 0.0)
                    for m in range(k + 1, SUB):
                        b[m][h - g] = b[m][h - g] - column * factors[m - k - 1]
                    r[h] = r[h] - spread(column) * scaled
            r[g] = jnp.where(lane >= row_index + start, r[g] * spread(lax.rsqrt(pivots)), 0.0)
    return rows


def exchange(ref, slots, send, recv, name, n, width=None):
    me = lax.axis_index(name)
    copies = []
    for k in range(1, n):
        other = lax.rem(me + k, n)
        part = ref if width is None else ref.at[pl.ds(pl.multiple_of(other * width, width), width)]
        copies.append(
            pltpu.make_async_remote_copy(
                src_ref=part,
                dst_ref=slots.at[k],
                send_sem=send.at[k],
                recv_sem=recv.at[k],
                device_id={name: other},
                device_id_type=MESH,
            )
        )
        copies[-1].start()
    return copies


def added(slots, name, n):
    me = lax.axis_index(name)
    acc = slots[me]
    for i in range(1, n):
        acc = acc + slots[lax.rem(me - i + n, n)]
    return acc


def finish_kernel(panel, offsets, axes, scale, damping, sens, prior, *rest):
    parts = rest[: len(offsets)]
    scene_rows, factor, info, spread_sens, out = rest[len(offsets) : len(offsets) + 5]
    mine, near, wide_slots, whole, written, s1, r1, s2, r2, s3, r3 = rest[len(offsets) + 5 :]
    barrier = pltpu.get_barrier_semaphore()
    for name, n in axes:
        me = lax.axis_index(name)
        for k in range(1, n):
            pl.semaphore_signal(
                barrier, inc=1, device_id={name: lax.rem(me + k, n)}, device_id_type=MESH
            )
    mine[...] = factor_scenes(panel, offsets, damping, sens, parts, out, info, spread_sens)
    rows = pltpu.make_async_copy(out, scene_rows, written)
    rows.start()
    pl.semaphore_wait(barrier, sum(n - 1 for _, n in axes))
    (tie, n), (scene, groups) = axes
    chunk = mine.shape[0] // n
    me = lax.axis_index(tie)
    own = pl.ds(pl.multiple_of(me * chunk, chunk), chunk)
    near[0] = mine[own]
    first = exchange(mine, near, s1, r1, tie, n, chunk)
    for copy in first:
        copy.wait_recv()
    wide_slots[0] = added(near, tie, n)
    second = exchange(wide_slots.at[0], wide_slots, s2, r2, scene, groups)
    for copy in second:
        copy.wait_recv()
    whole[own] = added(wide_slots, scene, groups)
    third = []
    for k in range(1, n):
        third.append(
            pltpu.make_async_remote_copy(
                src_ref=whole.at[own],
                dst_ref=whole.at[own],
                send_sem=s3.at[k],
                recv_sem=r3.at[k],
                device_id={tie: lax.rem(me + k, n)},
                device_id_type=MESH,
            )
        )
        third[-1].start()
    for copy in third:
        copy.wait_recv()
    shared = factor.shape[0]
    lane = lax.broadcasted_iota(jnp.int32, (shared, shared), 1)
    row = lax.broadcasted_iota(jnp.int32, (shared, shared), 0)
    value = jnp.concatenate([whole[:, :shared], whole[:, shared:]], 0)
    value = value * scale + jnp.where(lane == row, prior[...], 0.0)
    factor[...] = jnp.concatenate(eliminate([value], 0)[0], 0)
    for copy in first + second + third:
        copy.wait_send()
    rows.wait()


def factor_scenes(panel, offsets, damping, sens, parts, out, info, spread_sens):
    own, width, _ = info.shape
    spline = out.shape[1]
    half = width // 2
    beyond = width - spline
    for q in range(own):
        wide = jnp.concatenate([sens[q], jnp.zeros((spline, beyond), BF16)], 1)
        spread_sens[q] = jnp.concatenate([wide, jnp.zeros((beyond, width), BF16)], 0)
    row_index = lax.broadcasted_iota(jnp.int32, (width, width), 0)
    lane = lax.broadcasted_iota(jnp.int32, (width, width), 1)
    on_diagonal = (row_index == lane) & (row_index < spline)
    across = lane[:half, :half] - row_index[:half, :half]
    for q in range(own):
        held = [
            (part, q - offset, part.shape[0] // width)
            for offset, part in zip(offsets, parts)
            if offset <= q < offset + part.shape[0] // width
        ]
        packed = sum(part[at * width : (at + 1) * width] for part, at, _ in held)
        diagonal = sum(part[size * width + at : size * width + at + 1] for part, at, size in held)
        side, both = packed[:half], packed[half:]
        upper = jnp.where(across > 0, both, 0.0)
        first = jnp.where(across >= 0, both, upper.T)
        lower = jnp.where(across < 0, both, 0.0)
        last = lower + jnp.where(across == 0, diagonal, lower.T)
        top = jnp.concatenate([first, side], 1)
        bottom = jnp.concatenate([side.T, last], 1)
        whole = jnp.concatenate([top, bottom], 0)
        s = spread_sens[q]
        mixed = whole + sum(
            jnp.dot(piece, s, preferred_element_type=F32) for piece in two_parts(whole)
        )
        result = mixed + sum(over_rows(s, piece) for piece in two_parts(mixed))
        info[q] = result + jnp.where(on_diagonal, damping[q], 0.0)
    for start in range(0, spline, panel):
        base = start // LANES * LANES
        panels = [info[q, start : start + panel, base:] for q in range(own)]
        rows = eliminate(panels, start - base)
        if base:
            out[:, start : start + panel, :base] = jnp.zeros((own, panel, base), F32)
        after = start + panel
        for q in range(own):
            block = jnp.concatenate(rows[q], 0)
            out[q, start : start + panel, base:] = block
            high, low = two_parts(block)
            left = jnp.concatenate([high, high, low], 0)
            right = jnp.concatenate([high, low, high], 0)
            for top in range(after // LANES * LANES, width, LANES):
                skip = max(after - top, 0)
                update = over_rows(left[:, top - base : top - base + LANES], right[:, top - base :])
                info[q, top + skip : top + LANES, top:] -= update[skip:]
    total = info[0, spline:, half:]
    for q in range(1, own):
        total = total + info[q, spline:, half:]
    total = total[:, spline - half :]
    middle = (width - spline) // 2
    return jnp.concatenate([total[:middle], total[middle:]], 1)


def finish(parts, sensitivity, damping, prior, width, axes):
    own = damping.shape[0]
    spline = sensitivity.shape[1]
    beyond = width - spline
    (_, n), (_, groups) = axes
    mine = lax.dynamic_slice_in_dim(sensitivity, lax.axis_index("tie") * own, own)
    offsets = [offset for offset, _ in parts]
    scale = 1.0 / (own * n * groups)
    block = (beyond // 2 // n, 2 * beyond)
    dma = pltpu.SemaphoreType.DMA
    return pl.pallas_call(
        functools.partial(finish_kernel, PANEL, offsets, axes, scale),
        in_specs=[pl.BlockSpec(memory_space=pltpu.SMEM)] + [VMEM] * (2 + len(parts)),
        out_specs=[pl.BlockSpec(memory_space=pl.ANY), VMEM],
        scratch_shapes=[
            pltpu.VMEM((own, width, width), F32),
            pltpu.VMEM((own, width, width), BF16),
            pltpu.VMEM((own, spline, width), F32),
            pltpu.VMEM((beyond // 2, 2 * beyond), F32),
            pltpu.VMEM((n,) + block, F32),
            pltpu.VMEM((groups,) + block, F32),
            pltpu.VMEM((beyond // 2, 2 * beyond), F32),
            dma,
            dma((n,)),
            dma((n,)),
            dma((groups,)),
            dma((groups,)),
            dma((n,)),
            dma((n,)),
        ],
        out_shape=[
            jax.ShapeDtypeStruct((own, spline, width), F32),
            jax.ShapeDtypeStruct((beyond, beyond), F32),
        ],
        compiler_params=pltpu.CompilerParams(
            collective_id=0, has_side_effects=True, vmem_limit_bytes=12 << 20
        ),
        name="finish",
    )(damping, mine, prior[None, :], *(part for _, part in parts))


def emit_kernel(rows, factor, rows_out, factor_out, sems):
    copies = [
        pltpu.make_async_copy(rows, rows_out, sems.at[0]),
        pltpu.make_async_copy(factor, factor_out, sems.at[1]),
    ]
    for copy in copies:
        copy.start()
    for copy in copies:
        copy.wait()


def emit(scene_rows, factor):
    anywhere = pl.BlockSpec(memory_space=pl.ANY)
    return pl.pallas_call(
        emit_kernel,
        in_specs=[anywhere] * 2,
        out_specs=[anywhere] * 2,
        scratch_shapes=[pltpu.SemaphoreType.DMA((2,))],
        out_shape=[jax.ShapeDtypeStruct(x.shape, x.dtype) for x in (scene_rows, factor)],
        compiler_params=pltpu.CompilerParams(vmem_limit_bytes=1 << 20),
        name="emit",
    )(scene_rows, factor)


def on_device(axes, tie_rows, point_counts, pattern, sensitivity, damping, prior):
    sizes = dict(axes)
    own = damping.shape[0]
    width = tie_rows.shape[2]
    parts = merged_sums(tie_rows, point_counts, pattern, own, sizes["tie"])
    return emit(*finish(parts, sensitivity, damping, prior, width, axes))


def solution(mesh):
    axes = (("tie", mesh.shape["tie"]), ("scene", mesh.shape["scene"]))
    placed = (
        P("tie", None, None),
        P("tie"),
        P("scene", "tie"),
        P("scene", None, None),
        P(("scene", "tie")),
        P(),
    )
    return jax.shard_map(
        functools.partial(on_device, axes),
        mesh=mesh,
        in_specs=placed,
        out_specs=(P(("scene", "tie"), None, None), P()),
        check_vma=False,
    )
```

```python
import functools

import jax
import jax.numpy as jnp
from jax import lax
from jax.experimental import pallas as pl
from jax.experimental.pallas import tpu as pltpu
from jax.sharding import PartitionSpec as P


MESH = pl.DeviceIdType.MESH
F32 = jnp.float32
BF16 = jnp.bfloat16
PANEL = 32
LANES = 128
SUB = 8
UNROLL = 8
DEPTH = 32
PIECES = 2
VMEM = pl.BlockSpec(memory_space=pltpu.VMEM)


def over_rows(a, b):
    return lax.dot_general(a, b, (((0,), (0,)), ((), ())), preferred_element_type=F32)


def gram_kernel(groups, own, pairs, counts, pattern, rows, *rest):
    outs = rest[: len(groups)]
    ring, acc, entries, arrived = rest[len(groups) :]
    depth, _, wide = ring.shape
    half = wide // 2
    total = pattern.shape[1]
    stride = 1 << (total - 1).bit_length()
    me = lax.axis_index("tie")

    def fetch(n):
        at = lax.rem(n, depth)
        block = entries[n] & (stride - 1)
        return pltpu.make_async_copy(rows.at[block], ring.at[at], arrived.at[at])

    def start_fetch(n, carry):
        fetch(n).start()
        return carry

    filled = jnp.int32(0)
    place = 0
    for hop, side, offset, size in groups:
        device = lax.rem(me // 2 + hop, pairs) * 2 + lax.rem(me + side, 2)

        def scan(q, n, device=device, offset=offset, place=place):
            scene = device * own + offset + q
            base = (place + q) * stride
            was = n
            for block in range(total):
                entries[n] = base + block
                n = n + pattern[scene, block]
            lax.fori_loop(jnp.minimum(was, depth), jnp.minimum(n, depth), start_fetch, 0)
            return n

        filled = lax.fori_loop(0, size, scan, filled)
        place += size
    acc[...] = jnp.zeros_like(acc)
    reach = lax.broadcasted_iota(jnp.int32, (2 * SUB, wide), 1)

    def step(it, carry):
        for u in range(UNROLL):
            n = it * UNROLL + u

            @pl.when(n < filled)
            def _(n=n):
                fetch(n).wait()

        for u in range(UNROLL):
            n = it * UNROLL + u
            at = jnp.minimum(n, filled - 1)
            entry = entries[at]
            keep = jnp.where(n < filled, 2 * counts[entry & (stride - 1)], 0)
            value = ring[lax.rem(at, depth)]
            mask = jnp.where(reach < keep, 1.0, 0.0).astype(BF16)
            kept = value.T * jnp.concatenate([mask] * (wide // (2 * SUB)), 0)
            top = jnp.dot(kept[:half], value, preferred_element_type=F32)
            bottom = jnp.dot(kept[half:], value[:, half:], preferred_element_type=F32)
            to = entry // stride
            acc[to, :half] += top[:, :half]
            acc[to, half : 2 * half] += top[:, half:]
            acc[to, 2 * half :] += bottom
        for u in range(UNROLL):
            n = it * UNROLL + u + depth

            @pl.when(n < filled)
            def _(n=n):
                fetch(n).start()

        return carry

    lax.fori_loop(0, (filled + UNROLL - 1) // UNROLL, step, 0)
    row = lax.broadcasted_iota(jnp.int32, (half, half), 0)
    lane = lax.broadcasted_iota(jnp.int32, (half, half), 1)
    place = 0
    for out, (_, _, _, size) in zip(outs, groups):
        diagonals = [None] * size
        for q in range(size):
            low = acc[place, 2 * half :]
            at = q * wide
            out[at : at + half] = acc[place, half : 2 * half]
            out[at + half : at + wide] = jnp.where(row <= lane, acc[place, :half], low)
            diagonals[q] = jnp.sum(jnp.where(row == lane, low, 0.0), 0, keepdims=True)
            place += 1
        diagonals += [jnp.zeros((1, half), F32)] * (out.shape[0] - size * wide - size)
        out[size * wide :] = jnp.concatenate(diagonals, 0)


def gram_sums(tie_rows, point_counts, pattern, groups, own, n):
    total, height, wide = tie_rows.shape
    half = wide // 2
    sizes = [group[3] for group in groups]
    most = sum(sizes)
    smem = pl.BlockSpec(memory_space=pltpu.SMEM)
    return pl.pallas_call(
        functools.partial(gram_kernel, groups, own, n // 2),
        in_specs=[smem, smem, pl.BlockSpec(memory_space=pl.ANY)],
        out_specs=[VMEM] * len(sizes),
        out_shape=[
            jax.ShapeDtypeStruct((size * wide + -(-size // SUB) * SUB, half), F32) for size in sizes
        ],
        scratch_shapes=[
            pltpu.VMEM((DEPTH, height, wide), BF16),
            pltpu.VMEM((most, 3 * half, half), F32),
            pltpu.SMEM((most * total + 1,), jnp.int32),
            pltpu.SemaphoreType.DMA((DEPTH,)),
        ],
        compiler_params=pltpu.CompilerParams(vmem_limit_bytes=16 << 20),
    )(point_counts, pattern, tie_rows)


def join_kernel(x, y, out):
    out[...] = x[...] + y[...]


def join(x, y):
    return pl.pallas_call(
        join_kernel,
        in_specs=[VMEM] * 2,
        out_specs=VMEM,
        out_shape=jax.ShapeDtypeStruct(x.shape, F32),
        compiler_params=pltpu.CompilerParams(vmem_limit_bytes=4 << 20),
        name="join",
    )(x, y)


def swap_cores(x, n):
    return lax.ppermute(x, "tie", [(t, t ^ 1) for t in range(n)])


def send_over(x, n, hop):
    pairs = n // 2
    return lax.ppermute(x, "tie", [(t, (t // 2 + hop) % pairs * 2 + t % 2) for t in range(n)])


def merged_sums(tie_rows, point_counts, pattern, own, n):
    size = own // PIECES
    parts = []
    tie_rows, point_counts, pattern = (
        pltpu.with_memory_space_constraint(x, pltpu.HBM) for x in (tie_rows, point_counts, pattern)
    )
    offsets = range(0, own, size)
    for hop in range(1, n // 2):
        groups = [(hop, side, offset, size) for side in (1, 0) for offset in offsets]
        sums = gram_sums(tie_rows, point_counts, pattern, groups, own, n)
        swapped = [swap_cores(theirs, n) for theirs in sums[: len(offsets)]]
        for offset, mine, theirs in zip(offsets, sums[len(offsets) :], swapped):
            both = join(mine, theirs)
            both, point_counts = lax.optimization_barrier((both, point_counts))
            parts.append((offset, send_over(both, n, hop)))
    groups = [(0, 1, offset, size) for offset in offsets] + [(0, 0, 0, own)]
    sums = gram_sums(tie_rows, point_counts, pattern, groups, own, n)
    swapped = [(o, swap_cores(theirs, n)) for o, theirs in zip(offsets, sums)]
    return [(0, sums[-1])] + swapped + parts


def two_parts(x):
    high = x.astype(BF16)
    return high, (x - high.astype(F32)).astype(BF16)


def eliminate(panels, first):
    height, wide = panels[0].shape
    tile = (SUB, LANES)
    count = height // SUB
    rows = [[p[SUB * h : SUB * (h + 1)] for h in range(count)] for p in panels]
    row_index = lax.broadcasted_iota(jnp.int32, (SUB, wide), 0)
    lane = lax.broadcasted_iota(jnp.int32, (SUB, wide), 1)
    tile_row = lax.broadcasted_iota(jnp.int32, tile, 0)
    below = [tile_row > k for k in range(SUB)]

    def spread(x):
        return x if wide == LANES else (jnp.concatenate([x] * (wide // LANES), 1) if wide > LANES else x[:, :wide])

    for g in range(count):
        start = first + SUB * g
        cols = [
            [[jnp.broadcast_to(r[h][:, start + m : start + m + 1], tile) for h in range(g, count)] for m in range(SUB)]
            for r in rows
        ]
        for q, r in enumerate(rows):
            b = cols[q]
            pivots = b[0][0]
            for k in range(SUB):
                inverse = 1.0 / b[k][0][k : k + 1]
                pivots = jnp.where(tile_row == k, b[k][0], pivots)
                scaled = r[g][k : k + 1] * spread(inverse)
                factors = [b[m][0][k : k + 1] * inverse for m in range(k + 1, SUB)]
                for h in range(g, count):
                    column = b[k][h - g]
                    if h == g:
                        if k == SUB - 1:
                            continue
                        column = jnp.where(below[k], column, 0.0)
                    for m in range(k + 1, SUB):
                        b[m][h - g] = b[m][h - g] - column * factors[m - k - 1]
                    r[h] = r[h] - spread(column) * scaled
            r[g] = jnp.where(lane >= row_index + start, r[g] * spread(lax.rsqrt(pivots)), 0.0)
    return rows


def exchange(ref, slots, send, recv, name, n, width=None):
    me = lax.axis_index(name)
    copies = []
    for k in range(1, n):
        other = lax.rem(me + k, n)
        part = ref if width is None else ref.at[pl.ds(pl.multiple_of(other * width, width), width)]
        copies.append(
            pltpu.make_async_remote_copy(
                src_ref=part,
                dst_ref=slots.at[k],
                send_sem=send.at[k],
                recv_sem=recv.at[k],
                device_id={name: other},
                device_id_type=MESH,
            )
        )
        copies[-1].start()
    return copies


def added(slots, name, n):
    me = lax.axis_index(name)
    acc = slots[me]
    for i in range(1, n):
        acc = acc + slots[lax.rem(me - i + n, n)]
    return acc


def finish_kernel(panel, offsets, axes, scale, damping, sens, prior, *rest):
    parts = rest[: len(offsets)]
    scene_rows, factor, info, spread_sens, out = rest[len(offsets) : len(offsets) + 5]
    mine, near, wide_slots, whole, written, s1, r1, s2, r2, s3, r3 = rest[len(offsets) + 5 :]
    barrier = pltpu.get_barrier_semaphore()
    for name, n in axes:
        me = lax.axis_index(name)
        for k in range(1, n):
            pl.semaphore_signal(
                barrier, inc=1, device_id={name: lax.rem(me + k, n)}, device_id_type=MESH
            )
    mine[...] = factor_scenes(panel, offsets, damping, sens, parts, out, info, spread_sens)
    rows = pltpu.make_async_copy(out, scene_rows, written)
    rows.start()
    pl.semaphore_wait(barrier, sum(n - 1 for _, n in axes))
    (tie, n), (scene, groups) = axes
    chunk = mine.shape[0] // n
    me = lax.axis_index(tie)
    own = pl.ds(pl.multiple_of(me * chunk, chunk), chunk)
    near[0] = mine[own]
    first = exchange(mine, near, s1, r1, tie, n, chunk)
    for copy in first:
        copy.wait_recv()
    wide_slots[0] = added(near, tie, n)
    second = exchange(wide_slots.at[0], wide_slots, s2, r2, scene, groups)
    for copy in second:
        copy.wait_recv()
    whole[own] = added(wide_slots, scene, groups)
    third = []
    for k in range(1, n):
        third.append(
            pltpu.make_async_remote_copy(
                src_ref=whole.at[own],
                dst_ref=whole.at[own],
                send_sem=s3.at[k],
                recv_sem=r3.at[k],
                device_id={tie: lax.rem(me + k, n)},
                device_id_type=MESH,
            )
        )
        third[-1].start()
    for copy in third:
        copy.wait_recv()
    shared = factor.shape[0]
    lane = lax.broadcasted_iota(jnp.int32, (shared, shared), 1)
    row = lax.broadcasted_iota(jnp.int32, (shared, shared), 0)
    value = jnp.concatenate([whole[:, :shared], whole[:, shared:]], 0)
    value = value * scale + jnp.where(lane == row, prior[...], 0.0)
    factor[...] = jnp.concatenate(eliminate([value], 0)[0], 0)
    for copy in first + second + third:
        copy.wait_send()
    rows.wait()


def factor_scenes(panel, offsets, damping, sens, parts, out, info, spread_sens):
    own, width, _ = info.shape
    spline = out.shape[1]
    half = width // 2
    beyond = width - spline
    for q in range(own):
        wide = jnp.concatenate([sens[q], jnp.zeros((spline, beyond), BF16)], 1)
        spread_sens[q] = jnp.concatenate([wide, jnp.zeros((beyond, width), BF16)], 0)
    row_index = lax.broadcasted_iota(jnp.int32, (width, width), 0)
    lane = lax.broadcasted_iota(jnp.int32, (width, width), 1)
    on_diagonal = (row_index == lane) & (row_index < spline)
    across = lane[:half, :half] - row_index[:half, :half]
    for q in range(own):
        held = [
            (part, q - offset, part.shape[0] // width)
            for offset, part in zip(offsets, parts)
            if offset <= q < offset + part.shape[0] // width
        ]
        packed = sum(part[at * width : (at + 1) * width] for part, at, _ in held)
        diagonal = sum(part[size * width + at : size * width + at + 1] for part, at, size in held)
        side, both = packed[:half], packed[half:]
        upper = jnp.where(across > 0, both, 0.0)
        first = jnp.where(across >= 0, both, upper.T)
        lower = jnp.where(across < 0, both, 0.0)
        last = lower + jnp.where(across == 0, diagonal, lower.T)
        top = jnp.concatenate([first, side], 1)
        bottom = jnp.concatenate([side.T, last], 1)
        whole = jnp.concatenate([top, bottom], 0)
        s = spread_sens[q]
        mixed = whole + sum(
            jnp.dot(piece, s, preferred_element_type=F32) for piece in two_parts(whole)
        )
        result = mixed + sum(over_rows(s, piece) for piece in two_parts(mixed))
        info[q] = result + jnp.where(on_diagonal, damping[q], 0.0)
    for start in range(0, spline, panel):
        base = start // LANES * LANES
        panels = [info[q, start : start + panel, base:] for q in range(own)]
        rows = eliminate(panels, start - base)
        if base:
            out[:, start : start + panel, :base] = jnp.zeros((own, panel, base), F32)
        after = start + panel
        for q in range(own):
            block = jnp.concatenate(rows[q], 0)
            out[q, start : start + panel, base:] = block
            high, low = two_parts(block)
            left = jnp.concatenate([high, high, low], 0)
            right = jnp.concatenate([high, low, high], 0)
            for top in range(after // LANES * LANES, width, LANES):
                skip = max(after - top, 0)
                update = over_rows(left[:, top - base : top - base + LANES], right[:, top - base :])
                info[q, top + skip : top + LANES, top:] -= update[skip:]
    total = info[0, spline:, half:]
    for q in range(1, own):
        total = total + info[q, spline:, half:]
    total = total[:, spline - half :]
    middle = (width - spline) // 2
    return jnp.concatenate([total[:middle], total[middle:]], 1)


def finish(parts, sensitivity, damping, prior, width, axes):
    own = damping.shape[0]
    spline = sensitivity.shape[1]
    beyond = width - spline
    (_, n), (_, groups) = axes
    mine = lax.dynamic_slice_in_dim(sensitivity, lax.axis_index("tie") * own, own)
    offsets = [offset for offset, _ in parts]
    scale = 1.0 / (own * n * groups)
    block = (beyond // 2 // n, 2 * beyond)
    dma = pltpu.SemaphoreType.DMA
    return pl.pallas_call(
        functools.partial(finish_kernel, PANEL, offsets, axes, scale),
        in_specs=[pl.BlockSpec(memory_space=pltpu.SMEM)] + [VMEM] * (2 + len(parts)),
        out_specs=[pl.BlockSpec(memory_space=pl.ANY), VMEM],
        scratch_shapes=[
            pltpu.VMEM((own, width, width), F32),
            pltpu.VMEM((own, width, width), BF16),
            pltpu.VMEM((own, spline, width), F32),
            pltpu.VMEM((beyond // 2, 2 * beyond), F32),
            pltpu.VMEM((n,) + block, F32),
            pltpu.VMEM((groups,) + block, F32),
            pltpu.VMEM((beyond // 2, 2 * beyond), F32),
            dma,
            dma((n,)),
            dma((n,)),
            dma((groups,)),
            dma((groups,)),
            dma((n,)),
            dma((n,)),
        ],
        out_shape=[
            jax.ShapeDtypeStruct((own, spline, width), F32),
            jax.ShapeDtypeStruct((beyond, beyond), F32),
        ],
        compiler_params=pltpu.CompilerParams(
            collective_id=0, has_side_effects=True, vmem_limit_bytes=12 << 20
        ),
        name="finish",
    )(damping, mine, prior[None, :], *(part for _, part in parts))


def emit_kernel(rows, factor, rows_out, factor_out, sems):
    own = rows.shape[0]
    copies = [pltpu.make_async_copy(factor, factor_out, sems.at[own])]
    for q in range(own):
        copies.append(pltpu.make_async_copy(rows.at[q], rows_out.at[q], sems.at[q]))
    for copy in copies:
        copy.start()
    for copy in copies:
        copy.wait()


def emit(scene_rows, factor):
    anywhere = pl.BlockSpec(memory_space=pl.ANY)
    return pl.pallas_call(
        emit_kernel,
        in_specs=[anywhere] * 2,
        out_specs=[anywhere] * 2,
        scratch_shapes=[pltpu.SemaphoreType.DMA((scene_rows.shape[0] + 1,))],
        out_shape=[jax.ShapeDtypeStruct(x.shape, x.dtype) for x in (scene_rows, factor)],
        compiler_params=pltpu.CompilerParams(vmem_limit_bytes=1 << 20),
        name="emit",
    )(scene_rows, factor)


def on_device(axes, tie_rows, point_counts, pattern, sensitivity, damping, prior):
    sizes = dict(axes)
    own = damping.shape[0]
    width = tie_rows.shape[2]
    parts = merged_sums(tie_rows, point_counts, pattern, own, sizes["tie"])
    return emit(*finish(parts, sensitivity, damping, prior, width, axes))


def solution(mesh):
    axes = (("tie", mesh.shape["tie"]), ("scene", mesh.shape["scene"]))
    placed = (
        P("tie", None, None),
        P("tie"),
        P("scene", "tie"),
        P("scene", None, None),
        P(("scene", "tie")),
        P(),
    )
    return jax.shard_map(
        functools.partial(on_device, axes),
        mesh=mesh,
        in_specs=placed,
        out_specs=(P(("scene", "tie"), None, None), P()),
        check_vma=False,
    )
```
